128 devices in a mesh: cuts: 32 (over x, y, core), tile: 4 (over z).
Axes of the slice: x: 4, y: 4, z: 4, core: 2. Of those that a mesh axis runs over, the one named last changes fastest.
Arguments:
- probes: float32 [32, 8, 16, 4, 128], P('cuts', None, None, 'tile'), may hold values from -6 to 6
- test_block: float32 [32, 8, 16, 4, 128], P('cuts', None, None, 'tile'), may hold values from -6 to 6
- band_edge: float32 [8, 4, 128], P(None, 'tile'), may hold values from -3 to 3
- slice_hop: float32 [8], replicated, may hold values from 0.5 to 40
- cross_hop: float32 [2, 8, 8], replicated, may hold values from -0.4 to 0.4
- deform: float32 [6, 8, 8], replicated, may hold values from -0.4 to 0.4
- strain_elastic: float32 [32, 16, 6, 32], P('cuts', 'tile'), may hold values from -1 to 1
- strain_ids: int32 [16], replicated, may hold values from 0 to 15, as said below
Outputs:
- moment_fields: float32 [2, 2, 32, 8, 16, 4, 128], P(None, None, 'cuts', None, None, 'tile')
- projected: float32 [4, 2, 16, 16], replicated
The draws below stay inside these ranges and needn't reach their ends.
Inputs may be any that keep to these rules, and one draw needn't show every extreme that they name: strain_ids is a permutation; subtile g belongs to index g // 4 of tile, and slots i belong to index i // 4. The 4 slots of one index of tile hold at most 2 subtiles belonging to any one index, and exactly 2 for some index.
All inputs are finite; a program needn't handle non-finite values.
Results may differ from the reference program's by a relative error of at most 0.0085.
Values sent between devices are 32-bit elements; how exact they have to be, the bound alone decides.
No kernel may reach another device: no remote copies, remote signals or barrier semaphores. Data moves between devices by JAX's collectives and lax.ppermute only.
A program may use at most 128 MiB of HBM per device.

```python
import math
import jax
import jax.numpy as jnp
import numpy as np
from jax import lax

BANDS = 8
PROBES = 16
PTS = 8
NMOM = 4
CX = 128
SUBC = 32
SLICES = 32
CYT = 4
NSUB = 4
NSUB_ALL = 16


def draw_strain_ids(key, part):
    sub_count = NSUB
    total = NSUB_ALL
    tile_count = total // sub_count
    key_shift, key_rank, key_order = jax.random.split(key, 3)
    shifts = jax.random.permutation(key_shift, tile_count)[:3]
    rank_keys = jax.random.split(key_rank, tile_count)
    position = jax.vmap(lambda single: jax.random.permutation(single, sub_count))(rank_keys)
    segment = jnp.where(position < sub_count // 2, 0, jnp.where(position < 3 * sub_count // 4, 1, 2))
    owners = (jnp.arange(tile_count)[:, None] - shifts[segment]) % tile_count
    shuffle = jax.random.permutation(key_order, total).reshape(tile_count, sub_count)
    ordering = owners * total + shuffle
    return jnp.argsort(ordering.reshape(-1)).astype(jnp.int32)


def levels(stream_key, extent, shards, low, largest):
    level = 1.0
    for dim, blocks in shards:
        draws = jax.random.uniform(jax.random.fold_in(jax.random.fold_in(stream_key, 6), dim), (blocks,), jnp.float32, low / len(shards), largest / len(shards))
        level = level * jnp.repeat(jnp.exp(draws), extent[dim] // blocks).reshape((-1,) + (1,) * (len(extent) - 1 - dim))
    return level


def gaussian(own_key, extent, width, reach, pieces=(), kind=jnp.bfloat16):
    entries = width * jax.random.normal(own_key, extent, jnp.float32)
    if pieces:
        entries = entries * levels(own_key, extent, pieces, -0.22, 0.18)
    return jnp.clip(entries, -reach, reach).astype(kind)


def setup_inputs(seed: int = 0) -> dict:
    streams_of = jax.random.split(jax.random.key(seed), 9)
    probes = gaussian(streams_of[0], (SLICES, BANDS, PROBES, CYT, CX), 1.0, 6.0, ((0, 32), (3, 4)), jnp.float32)
    test_block = gaussian(streams_of[1], (SLICES, BANDS, PROBES, CYT, CX), 1.0, 6.0, ((0, 32), (3, 4)), jnp.float32)
    band_edge = jnp.clip(jax.random.uniform(streams_of[2], (BANDS, CYT, CX), jnp.float32, -3.0, 3.0) * levels(streams_of[2], (BANDS, CYT, CX), ((1, 4),), -0.4, 0.0), -3.0, 3.0)
    slice_hop = jnp.clip(jnp.exp(jax.random.uniform(streams_of[3], (BANDS,), jnp.float32, math.log(0.5), math.log(40.0))), 0.5, 40.0)
    cross_hop = gaussian(streams_of[4], (2, BANDS, BANDS), 0.08, 0.4, (), jnp.float32)
    deform = gaussian(streams_of[5], (6, BANDS, BANDS), 0.08, 0.4, (), jnp.float32)
    strain_elastic = jnp.clip(jax.random.uniform(streams_of[6], (SLICES, NSUB_ALL, 6, SUBC), jnp.float32, -1.0, 1.0) * levels(streams_of[6], (SLICES, NSUB_ALL, 6, SUBC), ((0, 32), (1, 4)), -0.4, 0.0), -1.0, 1.0)
    strain_ids = draw_strain_ids(jax.random.fold_in(streams_of[8], 71), 0)
    return dict(probes=probes, test_block=test_block, band_edge=band_edge, slice_hop=slice_hop, cross_hop=cross_hop, deform=deform, strain_elastic=strain_elastic, strain_ids=strain_ids)


HIGHEST = lax.Precision.HIGHEST

def complex_times(former, latter):
    return jnp.stack([former[0] * latter[0] - former[1] * latter[1], former[0] * latter[1] + former[1] * latter[0]])

def complex_inverse(number):
    square = number[0] * number[0] + number[1] * number[1]
    return jnp.stack([number[0] / square, -number[1] / square])

def complex_power(base_value, exponent, bit_count):
    result = jnp.stack([jnp.ones_like(base_value[0]), jnp.zeros_like(base_value[0])])
    squared = base_value
    for bit_index in range(bit_count):
        bit_set = exponent // 2 ** bit_index % 2
        result = jnp.where(bit_set == 1, complex_times(result, squared), result)
        squared = complex_times(squared, squared)
    return result

def line_ratio(band_edge, slice_hop, real_part, imag_part):
    hopping = slice_hop[:, None, None]
    ratio_re = (real_part - band_edge) / hopping
    ratio_im = (imag_part + 0.0 * band_edge) / hopping
    disc_re = ratio_re * ratio_re - ratio_im * ratio_im - 4.0
    disc_im = 2.0 * ratio_re * ratio_im
    modulus = jnp.sqrt(disc_re * disc_re + disc_im * disc_im)
    root_re = jnp.sqrt(jnp.maximum(0.5 * (modulus + disc_re), 0.0))
    root_im = jnp.sqrt(jnp.maximum(0.5 * (modulus - disc_re), 0.0)) * jnp.where(disc_im >= 0.0, 1.0, -1.0)
    lower_re = 0.5 * (ratio_re - root_re)
    lower_im = 0.5 * (ratio_im - root_im)
    upper_re = 0.5 * (ratio_re + root_re)
    upper_im = 0.5 * (ratio_im + root_im)
    choose_low = lower_re * lower_re + lower_im * lower_im <= upper_re * upper_re + upper_im * upper_im
    alpha_re = jnp.where(choose_low, lower_re, upper_re)
    alpha_im = jnp.where(choose_low, lower_im, upper_im)
    return jnp.stack([-alpha_re, -alpha_im])

def line_kernel(decay_rate, slice_hop, length):
    bit_count = length.bit_length()
    exponents = jnp.arange(length + 1).reshape(-1, 1, 1, 1)
    powers = complex_power(decay_rate[:, None], exponents, bit_count)
    series = powers[:, :length] + powers[:, length:0:-1]
    unit_value = jnp.stack([jnp.ones_like(decay_rate[0]), jnp.zeros_like(decay_rate[0])])
    denominator = complex_times(unit_value - complex_times(decay_rate, decay_rate), unit_value - powers[:, length])
    leading = complex_times(-decay_rate / slice_hop[None, :, None, None], complex_inverse(denominator))
    profile = complex_times(leading[:, None], series)
    offsets = (np.arange(length)[:, None] - np.arange(length)[None, :]) % length
    return jnp.take(profile, jnp.asarray(offsets, dtype=jnp.int32), axis=1)

def apply_lines(kernel, amplitude):

    def contract(former, latter):
        return jnp.einsum('smbyx,mbpyx->sbpyx', former, latter, precision=HIGHEST)
    return jnp.stack([contract(kernel[0], amplitude[0]) - contract(kernel[1], amplitude[1]), contract(kernel[0], amplitude[1]) + contract(kernel[1], amplitude[0])])

def couple_cells(amplitude, cross_hop, strain_mix):
    widths = [(0, 0)] * 5
    toward_right = jnp.pad(amplitude[..., 1:], widths + [(0, 1)])
    toward_left = jnp.pad(amplitude[..., :-1], widths + [(1, 0)])
    upward = jnp.pad(amplitude[..., 1:, :], widths[:4] + [(0, 1), (0, 0)])
    downward = jnp.pad(amplitude[..., :-1, :], widths[:4] + [(1, 0), (0, 0)])
    hoppers = jnp.stack([cross_hop[0], cross_hop[0].T, cross_hop[1], cross_hop[1].T])
    nearby = jnp.stack([toward_right, toward_left, upward, downward])
    summed = jnp.einsum('dbc,dkscpyx->ksbpyx', hoppers, nearby, precision=HIGHEST)
    return summed + jnp.einsum('sbcyx,kscpyx->ksbpyx', strain_mix, amplitude, precision=HIGHEST)

def reference(probes, test_block, band_edge, slice_hop, cross_hop, deform, strain_elastic, strain_ids):
    slices = probes.shape[0]
    bands = probes.shape[1]
    rows_all = probes.shape[3]
    cols_all = probes.shape[4]
    placed = jnp.zeros_like(strain_elastic).at[:, strain_ids].set(strain_elastic)
    strain = jnp.transpose(placed, (0, 2, 1, 3)).reshape(slices, 6, rows_all, cols_all)
    symmetric = 0.5 * (deform + jnp.transpose(deform, (0, 2, 1)))
    strain_mix = jnp.einsum('skyx,kbc->sbcyx', strain, symmetric, precision=HIGHEST)
    source = jnp.stack([probes, jnp.zeros_like(probes)])
    moments = jnp.zeros((NMOM, 2) + probes.shape, jnp.float32)
    for point in range(PTS):
        angle = math.pi * (2 * point + 1) / PTS
        decay_rate = line_ratio(band_edge, slice_hop, math.cos(angle), math.sin(angle))
        kernel = line_kernel(decay_rate, slice_hop, slices)
        first_step = apply_lines(kernel, source)
        second_step = first_step + apply_lines(kernel, couple_cells(first_step, cross_hop, strain_mix))
        for order in range(NMOM):
            weight_re = math.cos((order + 1) * angle) / PTS
            weight_im = math.sin((order + 1) * angle) / PTS
            update = jnp.stack([weight_re * second_step[0] - weight_im * second_step[1], weight_re * second_step[1] + weight_im * second_step[0]])
            moments = moments.at[order].add(update)
    scale = (slices * bands * rows_all * cols_all) ** (-0.5)
    projected = jnp.einsum('sbqyx,nksbryx->nkqr', test_block, moments, precision=HIGHEST) * scale
    return (moments[:2], projected)
```

```python
import math

import jax
import jax.numpy as jnp
import numpy as np
from jax import lax
from jax.experimental import pallas as pl
from jax.experimental.pallas import tpu as pltpu
from jax.sharding import PartitionSpec as P

PTS = 8
NMOM = 4
HALF = PTS // 2
ALL = ("cuts", "tile")

BANDS = 8
CELLS = 128
ROWS = 4
SLICES = 32
PROBES = 16
STRAINS = 6
TERMS = STRAINS + 4
PLANE = ROWS * CELLS
DEVICES = SLICES * ROWS
CHUNK = 20
BACK = 4
NSUB = ROWS * ROWS
HIGHEST = lax.Precision.HIGHEST
VMEM_BYTES = 20 * 1024 * 1024


def pack_kernel(ids_ref, probes_ref, test_ref, strain_ref, edge_ref, out_ref):
    piece = lax.axis_index("cuts") % BANDS
    edge = edge_ref[pl.ds(piece, 1), :]
    strain = jnp.concatenate([strain_ref[:, slot, :] for slot in range(ROWS)], axis=1)
    shared = [
        jnp.concatenate([strain[3 * half : 3 * half + 3], edge], axis=0) for half in range(2)
    ]
    for probe in range(PROBES):
        half = probe // 4 % 2
        column = probes_ref[pl.ds(probe, BANDS, stride=PROBES), :]
        for band in range(BANDS):
            at = (band * PROBES + probe) * CHUNK
            out_ref[at : at + 8, :] = column
            out_ref[at + 8 : at + 12, :] = shared[half]
            first = band * PROBES + 8 * half
            out_ref[at + 12 : at + 20, :] = test_ref[first : first + 8, :]


def split(value):
    high = value.astype(jnp.bfloat16)
    low = (value - high.astype(jnp.float32)).astype(jnp.bfloat16)
    return high, low


def matmul(left, right):
    return jnp.dot(left, right, preferred_element_type=jnp.float32)


def main_kernel(
    scale,
    cosines,
    ids_ref,
    hop_ref,
    cross_ref,
    deform_ref,
    table_ref,
    mine_ref,
    other_ref,
    wave_ref,
    spread_ref,
    forth_ref,
    back_ref,
    cosine_ref,
    out_ref,
    place_ref,
    slots_ref,
    strain_ref,
    weights_ref,
    right_ref,
    waves_ref,
    field_ref,
    result_ref,
    source_ref,
    moment_ref,
    final_ref,
):
    half = lax.axis_index("cuts") % 2
    band = lax.axis_index("cuts") // 4
    lane = lax.broadcasted_iota(jnp.int32, (SLICES, CELLS), 1)

    for slot in range(NSUB):
        place_ref[ids_ref[slot]] = slot
    for holder in range(ROWS):
        for comp in range(3):
            rows = pl.ds(holder * CHUNK + 8 + comp, SLICES, stride=ROWS * CHUNK)
            a = mine_ref[rows, :]
            b = other_ref[rows, :]
            slots_ref[holder, comp * SLICES : (comp + 1) * SLICES, :] = jnp.where(half == 0, a, b)
            slots_ref[holder, (comp + 3) * SLICES : (comp + 4) * SLICES, :] = jnp.where(
                half == 0, b, a
            )
    group = lax.broadcasted_iota(jnp.int32, (STRAINS * SLICES, CELLS), 1) // (CELLS // ROWS)
    for row in range(ROWS):
        total = None
        for part in range(ROWS):
            slot = place_ref[row * ROWS + part]
            shift = ((part + ROWS - slot % ROWS) % ROWS) * (CELLS // ROWS)
            rolled = pltpu.roll(slots_ref[slot // ROWS], shift, 1)
            total = rolled if total is None else jnp.where(group == part, rolled, total)
        strain_ref[:, row * CELLS : (row + 1) * CELLS] = total

    source_band = lax.broadcasted_iota(jnp.int32, (1, SLICES * BANDS), 1) % BANDS
    for term in range(TERMS):
        line = jnp.zeros((1, SLICES * BANDS), jnp.float32)
        for src in range(BANDS):
            if term < STRAINS:
                entry = 0.5 * (deform_ref[term, band, src] + deform_ref[term, src, band])
            else:
                axis = (term - STRAINS) // 2
                if (term - STRAINS) % 2 == 0:
                    entry = cross_ref[axis, band, src]
                else:
                    entry = cross_ref[axis, src, band]
            line = jnp.where(source_band == src, entry, line)
        high, low = split(spread_ref[...] * line)
        at = slice(term * SLICES, (term + 1) * SLICES)
        weights_ref[at, 0:256] = high
        weights_ref[at, 256:512] = high
        weights_ref[at, 512:768] = low

    for s in range(SLICES):
        for row in range(ROWS):
            at = (s * ROWS + row) * CHUNK
            field_ref[s * BANDS : (s + 1) * BANDS, row * CELLS : (row + 1) * CELLS] = mine_ref[
                at : at + BANDS, :
            ]
    high, low = split(field_ref[:, 0:PLANE])
    right_ref[0:256, 0:PLANE] = high
    right_ref[256:512, 0:PLANE] = low
    right_ref[512:768, 0:PLANE] = high
    waves = matmul(wave_ref[...], right_ref[:, 0:PLANE])
    for row in range(ROWS):
        waves_ref[row] = waves[:, row * CELLS : (row + 1) * CELLS]

    sub = lax.broadcasted_iota(jnp.int32, (BANDS, CELLS), 0)
    hop = jnp.full((BANDS, CELLS), 2.0 * hop_ref[0], jnp.float32)
    for b in range(1, BANDS):
        hop = jnp.where(sub == b, 2.0 * hop_ref[b], hop)
    own_hop = 2.0 * hop_ref[band]
    moment_ref[...] = jnp.zeros_like(moment_ref)

    def point(j, _):
        z_re = table_ref[0, j]
        z_im = table_ref[1, j]
        square = z_im * z_im
        for row in range(ROWS):
            lanes = slice(row * CELLS, (row + 1) * CELLS)
            lanes_im = slice(PLANE + row * CELLS, PLANE + (row + 1) * CELLS)
            gap = z_re - mine_ref[pl.ds(row * CHUNK + 11, BANDS, stride=ROWS * CHUNK), :]
            for freq in range(SLICES // 2 + 1):
                u = gap + hop * cosines[freq]
                inverse = 1.0 / (u * u + square)
                g_re = u * inverse
                g_im = -z_im * inverse
                both = (freq, freq + SLICES // 2) if 0 < freq < SLICES // 2 else (freq,)
                for wave in both:
                    at = slice(wave * BANDS, (wave + 1) * BANDS)
                    value = waves_ref[row, at, :]
                    field_ref[at, lanes] = g_re * value
                    field_ref[at, lanes_im] = g_im * value
        high, low = split(field_ref[...])
        right_ref[0:256, :] = high
        right_ref[256:512, :] = low
        right_ref[512:768, :] = high
        result_ref[...] = matmul(weights_ref[...], right_ref[...])

        for part in range(2):
            for row in range(ROWS):
                at = part * PLANE + row * CELLS
                lanes = slice(at, at + CELLS)
                total = None
                for comp in range(STRAINS):
                    rows = slice(comp * SLICES, (comp + 1) * SLICES)
                    value = strain_ref[rows, row * CELLS : (row + 1) * CELLS] * result_ref[
                        rows, lanes
                    ]
                    total = value if total is None else total + value
                from_right = pltpu.roll(result_ref[192:224, lanes], CELLS - 1, 1)
                from_left = pltpu.roll(result_ref[224:256, lanes], 1, 1)
                total = total + jnp.where(lane < CELLS - 1, from_right, 0.0)
                total = total + jnp.where(lane > 0, from_left, 0.0)
                if row < ROWS - 1:
                    total = total + result_ref[256:288, at + CELLS : at + 2 * CELLS]
                if row > 0:
                    total = total + result_ref[288:320, at - CELLS : at]
                high, low = split(total)
                source_ref[0:32, lanes] = high
                source_ref[32:64, lanes] = low
                source_ref[64:96, lanes] = high
        result_ref[0:32, :] = matmul(forth_ref[...], source_ref[:, 0 : 2 * PLANE])

        for row in range(ROWS):
            lanes = slice(row * CELLS, (row + 1) * CELLS)
            lanes_im = slice(PLANE + row * CELLS, PLANE + (row + 1) * CELLS)
            edge = mine_ref[pl.ds((band * ROWS + row) * CHUNK + 11, 1), :]
            u = (z_re - edge) + own_hop * cosine_ref[...]
            inverse = 1.0 / (u * u + square)
            g_re = u * inverse
            g_im = -z_im * inverse
            a_re = result_ref[0:32, lanes] + waves_ref[row, pl.ds(band, SLICES, stride=BANDS), :]
            a_im = result_ref[0:32, lanes_im]
            v_re = g_re * a_re - g_im * a_im
            v_im = g_re * a_im + g_im * a_re
            for order in range(NMOM):
                at = slice(order * PLANE + row * CELLS, order * PLANE + (row + 1) * CELLS)
                moment_ref[:, at] += (
                    table_ref[2 + order, j] * v_re - table_ref[2 + NMOM + order, j] * v_im
                )
        return 0

    lax.fori_loop(0, HALF, point, 0)

    high, low = split(moment_ref[...])
    source_ref[0:32, :] = high
    source_ref[32:64, :] = low
    source_ref[64:96, :] = high
    final = matmul(back_ref[...], source_ref[...])
    for order in range(NMOM):
        for row in range(ROWS):
            at = order * PLANE + row * CELLS
            value = final[:, at : at + CELLS]
            final_ref[order * ROWS + row] = value
            if order < 2:
                out_ref[pl.ds(row * BACK + order, SLICES, stride=ROWS * BACK), :] = value

    zero = jnp.zeros((8, CELLS), jnp.float32)
    near = [zero] * NMOM
    far = [zero] * NMOM
    for s in range(SLICES):
        for row in range(ROWS):
            at = (s * ROWS + row) * CHUNK + 12
            test_near = mine_ref[at : at + 8, :]
            test_far = other_ref[at : at + 8, :]
            for order in range(NMOM):
                value = final_ref[order * ROWS + row, s : s + 1, :]
                near[order] = near[order] + test_near * value
                far[order] = far[order] + test_far * value
    stack = []
    for order in range(NMOM):
        stack.append(jnp.where(half == 0, near[order], far[order]))
        stack.append(jnp.where(half == 0, far[order], near[order]))
    sums = lax.dot_general(
        jnp.full((8, CELLS), scale, jnp.float32),
        jnp.concatenate(stack, axis=0),
        (((1,), (1,)), ((), ())),
        precision=HIGHEST,
        preferred_element_type=jnp.float32,
    )
    line = jnp.concatenate([sums, jnp.zeros_like(sums)], axis=1)[0:1]
    out_ref[pl.ds(2, DEVICES, stride=BACK), :] = jnp.broadcast_to(line, (DEVICES, CELLS))


def gather_kernel(blocks_ref, fields_ref, projected_ref):
    total = None
    for band in range(BANDS):
        first = band * PROBES * BACK
        for order in range(2):
            fields_ref[order, 0, band * PROBES : (band + 1) * PROBES, :] = blocks_ref[
                pl.ds(first + order, PROBES, stride=BACK), :
            ]
        part = blocks_ref[pl.ds(first + 2, PROBES, stride=BACK), :]
        total = part if total is None else total + part
    turned = total.T
    for order in range(2):
        fields_ref[order, 1] = jnp.zeros((BANDS * PROBES, CELLS), jnp.float32)
    for order in range(NMOM):
        projected_ref[order, 0] = turned[order * PROBES : (order + 1) * PROBES, :]
        projected_ref[order, 1] = jnp.zeros((PROBES, PROBES), jnp.float32)


def transform():
    s = np.arange(SLICES)
    rows = []
    for freq in range(SLICES // 2 + 1):
        norm = 1.0 if freq in (0, SLICES // 2) else 2.0
        rows.append(np.sqrt(norm / SLICES) * np.cos(2 * np.pi * freq * s / SLICES))
    for freq in range(1, SLICES // 2):
        rows.append(np.sqrt(2.0 / SLICES) * np.sin(2 * np.pi * freq * s / SLICES))
    return np.array(rows)


def split_constant(matrix):
    matrix = matrix.astype(np.float32)
    high = matrix.astype(jnp.bfloat16)
    low = (matrix - high.astype(np.float32)).astype(jnp.bfloat16)
    return jnp.asarray(np.concatenate([high, high, low], axis=1))


def constants():
    wave = transform()
    freqs = np.concatenate([np.arange(SLICES // 2 + 1), np.arange(1, SLICES // 2)])
    cosine = np.cos(2 * np.pi * freqs / SLICES)
    spread = np.repeat(wave.T, BANDS, axis=1)
    angles = np.pi * (2 * np.arange(HALF) + 1) / PTS
    orders = np.arange(1, NMOM + 1)[:, None]
    table = np.concatenate(
        [
            np.cos(angles)[None],
            np.sin(angles)[None],
            2.0 / PTS * np.cos(orders * angles),
            2.0 / PTS * np.sin(orders * angles),
        ]
    )
    return (
        [float(c) for c in cosine],
        jnp.asarray(table, jnp.float32),
        split_constant(np.kron(wave, np.eye(BANDS))),
        jnp.asarray(spread, jnp.float32),
        split_constant(wave),
        split_constant(wave.T),
        jnp.asarray(np.repeat(cosine[:, None], CELLS, axis=1), jnp.float32),
    )


def vmem():
    return pl.BlockSpec(memory_space=pltpu.VMEM)


def smem():
    return pl.BlockSpec(memory_space=pltpu.SMEM)


def shape(*dims):
    return jax.ShapeDtypeStruct(dims, jnp.float32)


def params():
    return pltpu.CompilerParams(vmem_limit_bytes=VMEM_BYTES)


def exchange(blocks, rows):
    wide = blocks.reshape(DEVICES, rows // 4, 4, CELLS)
    wide = lax.all_to_all(wide, ALL, split_axis=0, concat_axis=0, tiled=True)
    return wide.reshape(DEVICES * rows, CELLS)


def on_device(
    probes, test_block, band_edge, slice_hop, cross_hop, deform, strain_elastic, strain_ids
):
    cut_count = lax.axis_size("cuts")
    outgoing = pl.pallas_call(
        pack_kernel,
        out_shape=shape(DEVICES * CHUNK, CELLS),
        in_specs=[smem()] + [vmem()] * 4,
        out_specs=vmem(),
        compiler_params=params(),
        name="pack",
    )(
        strain_ids,
        probes.reshape(BANDS * PROBES, CELLS),
        test_block.reshape(BANDS * PROBES, CELLS),
        jnp.transpose(strain_elastic[0], (1, 0, 2)),
        band_edge.reshape(BANDS, CELLS),
    )
    mine = exchange(outgoing, CHUNK)
    other = lax.ppermute(mine, "cuts", [(i, i ^ 1) for i in range(cut_count)])
    scale = (cut_count * BANDS * ROWS * CELLS) ** (-0.5)
    cosines, table, *matrices = constants()

    def main(*refs):
        main_kernel(scale, cosines, *refs)

    blocks = pl.pallas_call(
        main,
        out_shape=shape(DEVICES * BACK, CELLS),
        in_specs=[smem()] * 5 + [vmem()] * 7,
        out_specs=vmem(),
        scratch_shapes=[
            pltpu.SMEM((NSUB,), jnp.int32),
            pltpu.VMEM((ROWS, STRAINS * SLICES, CELLS), jnp.float32),
            pltpu.VMEM((STRAINS * SLICES, PLANE), jnp.float32),
            pltpu.VMEM((TERMS * SLICES, 3 * SLICES * BANDS), jnp.bfloat16),
            pltpu.VMEM((3 * SLICES * BANDS, 2 * PLANE), jnp.bfloat16),
            pltpu.VMEM((ROWS, SLICES * BANDS, CELLS), jnp.float32),
            pltpu.VMEM((SLICES * BANDS, 2 * PLANE), jnp.float32),
            pltpu.VMEM((TERMS * SLICES, 2 * PLANE), jnp.float32),
            pltpu.VMEM((3 * SLICES, NMOM * PLANE), jnp.bfloat16),
            pltpu.VMEM((SLICES, NMOM * PLANE), jnp.float32),
            pltpu.VMEM((NMOM * ROWS, SLICES, CELLS), jnp.float32),
        ],
        compiler_params=params(),
        name="solve",
    )(strain_ids, slice_hop, cross_hop, deform, table, mine, other, *matrices)
    fields, projected = pl.pallas_call(
        gather_kernel,
        out_shape=(shape(2, 2, BANDS * PROBES, CELLS), shape(NMOM, 2, PROBES, PROBES)),
        in_specs=[vmem()],
        out_specs=(vmem(), vmem()),
        compiler_params=params(),
        name="gather",
    )(exchange(blocks, BACK))
    return fields.reshape(2, 2, 1, BANDS, PROBES, 1, CELLS), projected


def solution(mesh):
    placed = (
        P("cuts", None, None, "tile", None),
        P("cuts", None, None, "tile", None),
        P(None, "tile", None),
        P(),
        P(),
        P(),
        P("cuts", "tile", None, None),
        P(),
    )
    return jax.shard_map(
        on_device,
        mesh=mesh,
        in_specs=placed,
        out_specs=(P(None, None, "cuts", None, None, "tile", None), P()),
        check_vma=False,
    )
```

```python
import math

import jax
import jax.numpy as jnp
import numpy as np
from jax import lax
from jax.experimental import pallas as pl
from jax.experimental.pallas import tpu as pltpu
from jax.sharding import PartitionSpec as P

PTS = 8
NMOM = 4
HALF = PTS // 2
ALL = ("cuts", "tile")

BANDS = 8
CELLS = 128
ROWS = 4
SLICES = 32
PROBES = 16
STRAINS = 6
TERMS = STRAINS + 4
PLANE = ROWS * CELLS
DEVICES = SLICES * ROWS
CHUNK = 20
BACK = 3
NSUB = ROWS * ROWS
HIGHEST = lax.Precision.HIGHEST
VMEM_BYTES = 20 * 1024 * 1024


def pack_kernel(
    probes_hbm,
    test_hbm,
    strain_hbm,
    edge_hbm,
    out_ref,
    probes_ref,
    test_ref,
    strain_ref,
    edge_ref,
    done,
):
    pairs = (
        (probes_hbm, probes_ref),
        (test_hbm, test_ref),
        (strain_hbm, strain_ref),
        (edge_hbm, edge_ref),
    )
    copies = [pltpu.make_async_copy(*pair, done.at[i]) for i, pair in enumerate(pairs)]
    for copy in copies:
        copy.start()
    copies[0].wait()
    for probe in range(PROBES):
        column = probes_ref[pl.ds(probe, BANDS, stride=PROBES), :]
        for band in range(BANDS):
            at = (band * PROBES + probe) * CHUNK
            out_ref[at : at + 8, :] = column
    copies[1].wait()
    for probe in range(PROBES):
        for band in range(BANDS):
            at = (band * PROBES + probe) * CHUNK
            first = band * PROBES + 8 * (probe // 4 % 2)
            out_ref[at + 12 : at + 20, :] = test_ref[first : first + 8, :]
    copies[2].wait()
    copies[3].wait()
    piece = lax.axis_index("cuts") % BANDS
    edge = edge_ref[pl.ds(piece, 1), :]
    strain = jnp.concatenate([strain_ref[:, slot, :] for slot in range(ROWS)], axis=1)
    for half in range(2):
        shared = jnp.concatenate([strain[3 * half : 3 * half + 3], edge], axis=0)
        for probe in range(PROBES):
            if probe // 4 % 2 == half:
                for band in range(BANDS):
                    at = (band * PROBES + probe) * CHUNK
                    out_ref[at + 8 : at + 12, :] = shared


def split(value):
    high = value.astype(jnp.bfloat16)
    low = (value - high.astype(jnp.float32)).astype(jnp.bfloat16)
    return high, low


def matmul(left, right):
    return jnp.dot(left, right, preferred_element_type=jnp.float32)


def prepare_kernel(
    hop_ref,
    cross_ref,
    deform_ref,
    mine_ref,
    wave_ref,
    spread_ref,
    cosine_ref,
    weights_ref,
    waves_ref,
    hop_out_ref,
    shift_ref,
    field_ref,
):
    band = lax.axis_index("cuts") // 4

    for s in range(0, SLICES, 2):
        for row in range(ROWS):
            pair = [
                mine_ref[((s + i) * ROWS + row) * CHUNK : ((s + i) * ROWS + row) * CHUNK + 8, :]
                for i in range(2)
            ]
            high, low = split(jnp.concatenate(pair, axis=0))
            lanes = slice(row * CELLS, (row + 1) * CELLS)
            at = s * BANDS
            field_ref[at : at + 16, lanes] = high
            field_ref[256 + at : 272 + at, lanes] = low
            field_ref[512 + at : 528 + at, lanes] = high
    waves = matmul(wave_ref[...], field_ref[...])
    for row in range(ROWS):
        waves_ref[row] = waves[:, row * CELLS : (row + 1) * CELLS]

    source_band = lax.broadcasted_iota(jnp.int32, (1, SLICES * BANDS), 1) % BANDS
    for term in range(TERMS):
        line = jnp.zeros((1, SLICES * BANDS), jnp.float32)
        for src in range(BANDS):
            if term < STRAINS:
                entry = 0.5 * (deform_ref[term, band, src] + deform_ref[term, src, band])
            else:
                axis = (term - STRAINS) // 2
                if (term - STRAINS) % 2 == 0:
                    entry = cross_ref[axis, band, src]
                else:
                    entry = cross_ref[axis, src, band]
            line = jnp.where(source_band == src, entry, line)
        high, low = split(spread_ref[...] * line)
        at = slice(term * SLICES, (term + 1) * SLICES)
        weights_ref[at, 0:256] = high
        weights_ref[at, 256:512] = high
        weights_ref[at, 512:768] = low

    sub = lax.broadcasted_iota(jnp.int32, (BANDS, CELLS), 0)
    hop = jnp.full((BANDS, CELLS), 2.0 * hop_ref[0], jnp.float32)
    for b in range(1, BANDS):
        hop = jnp.where(sub == b, 2.0 * hop_ref[b], hop)
    hop_out_ref[...] = hop
    shift_ref[...] = 2.0 * hop_ref[band] * cosine_ref[...]


def point_scalar(values, j):
    out = jnp.float32(values[0])
    for i in range(1, HALF):
        out = jnp.where(j == i, jnp.float32(values[i]), out)
    return out


def main_kernel(
    scale,
    cosines,
    table,
    ids_ref,
    mine_ref,
    other_ref,
    weights_ref,
    waves_ref,
    hop_ref,
    shift_ref,
    forth_ref,
    back_ref,
    out_ref,
    place_ref,
    slots_ref,
    strain_ref,
    right_ref,
    result_ref,
    source_ref,
    moment_ref,
    final_ref,
):
    half = lax.axis_index("cuts") % 2
    band = lax.axis_index("cuts") // 4
    lane = lax.broadcasted_iota(jnp.int32, (SLICES, CELLS), 1)

    for slot in range(NSUB):
        place_ref[ids_ref[slot]] = slot
    for holder in range(ROWS):
        for comp in range(3):
            rows = pl.ds(holder * CHUNK + 8 + comp, SLICES, stride=ROWS * CHUNK)
            a = mine_ref[rows, :]
            b = other_ref[rows, :]
            slots_ref[holder, comp * SLICES : (comp + 1) * SLICES, :] = jnp.where(half == 0, a, b)
            slots_ref[holder, (comp + 3) * SLICES : (comp + 4) * SLICES, :] = jnp.where(
                half == 0, b, a
            )
    group = lax.broadcasted_iota(jnp.int32, (STRAINS * SLICES, CELLS), 1) // (CELLS // ROWS)
    for row in range(ROWS):
        total = None
        for part in range(ROWS):
            slot = place_ref[row * ROWS + part]
            shift = ((part + ROWS - slot % ROWS) % ROWS) * (CELLS // ROWS)
            rolled = pltpu.roll(slots_ref[slot // ROWS], shift, 1)
            total = rolled if total is None else jnp.where(group == part, rolled, total)
        strain_ref[:, row * CELLS : (row + 1) * CELLS] = total

    moment_ref[...] = jnp.zeros_like(moment_ref)
    hop = hop_ref[...]

    def point(j, _):
        z_re, z_im = point_scalar(table[0], j), point_scalar(table[1], j)
        square = z_im * z_im
        for row in range(ROWS):
            at_re = row * 2 * CELLS
            gap = z_re - mine_ref[pl.ds(row * CHUNK + 11, BANDS, stride=ROWS * CHUNK), :]
            for pair in range(SLICES // 2):
                parts = []
                for wave in (2 * pair, 2 * pair + 1):
                    if parts and cosines[wave] == cosines[wave - 1]:
                        parts.append(parts[0])
                        continue
                    u = gap + hop * cosines[wave]
                    inverse = 1.0 / (u * u + square)
                    parts.append((u * inverse, -z_im * inverse))
                rows = slice(pair * 16, pair * 16 + 16)
                value = waves_ref[row, rows, :]
                for part in range(2):
                    factor = jnp.concatenate([parts[0][part], parts[1][part]], axis=0)
                    high, low = split(factor * value)
                    lanes = slice(at_re + part * CELLS, at_re + (part + 1) * CELLS)
                    right_ref[rows, lanes] = high
                    right_ref[pair * 16 + 256 : pair * 16 + 272, lanes] = low
                    right_ref[pair * 16 + 512 : pair * 16 + 528, lanes] = high
            lanes = slice(at_re, at_re + 2 * CELLS)
            result_ref[:, lanes] = matmul(weights_ref[...], right_ref[:, lanes])

        for row in range(ROWS):
            for part in range(2):
                at = (2 * row + part) * CELLS
                lanes = slice(at, at + CELLS)
                total = None
                for comp in range(STRAINS):
                    rows = slice(comp * SLICES, (comp + 1) * SLICES)
                    value = strain_ref[rows, row * CELLS : (row + 1) * CELLS] * result_ref[
                        rows, lanes
                    ]
                    total = value if total is None else total + value
                from_right = pltpu.roll(result_ref[192:224, lanes], CELLS - 1, 1)
                from_left = pltpu.roll(result_ref[224:256, lanes], 1, 1)
                total = total + jnp.where(lane < CELLS - 1, from_right, 0.0)
                total = total + jnp.where(lane > 0, from_left, 0.0)
                if row < ROWS - 1:
                    total = total + result_ref[256:288, at + 2 * CELLS : at + 3 * CELLS]
                if row > 0:
                    total = total + result_ref[288:320, at - 2 * CELLS : at - CELLS]
                high, low = split(total)
                source_ref[0:32, lanes] = high
                source_ref[32:64, lanes] = low
                source_ref[64:96, lanes] = high
        result_ref[0:32, :] = matmul(forth_ref[...], source_ref[:, 0 : 2 * PLANE])

        for row in range(ROWS):
            at = row * 2 * CELLS
            edge = mine_ref[pl.ds((band * ROWS + row) * CHUNK + 11, 1), :]
            u = (z_re - edge) + shift_ref[...]
            inverse = 1.0 / (u * u + square)
            g_re = u * inverse
            g_im = -z_im * inverse
            a_re = result_ref[0:32, at : at + CELLS]
            a_re = a_re + waves_ref[row, pl.ds(band, SLICES, stride=BANDS), :]
            a_im = result_ref[0:32, at + CELLS : at + 2 * CELLS]
            v_re = g_re * a_re - g_im * a_im
            v_im = g_re * a_im + g_im * a_re
            for order in range(NMOM):
                lanes = slice(order * PLANE + row * CELLS, order * PLANE + (row + 1) * CELLS)
                w_re = point_scalar(table[2 + order], j)
                w_im = point_scalar(table[2 + NMOM + order], j)
                moment_ref[:, lanes] += w_re * v_re - w_im * v_im
        return 0

    lax.fori_loop(0, HALF, point, 0)

    high, low = split(moment_ref[...])
    source_ref[0:32, :] = high
    source_ref[32:64, :] = low
    source_ref[64:96, :] = high
    final = matmul(back_ref[...], source_ref[...])
    for order in range(NMOM):
        for row in range(ROWS):
            at = order * PLANE + row * CELLS
            value = final[:, at : at + CELLS]
            final_ref[order * ROWS + row] = value
            if order < 2:
                out_ref[pl.ds(row * BACK + order, SLICES, stride=ROWS * BACK), :] = value

    zero = jnp.zeros((8, CELLS), jnp.float32)
    near = [zero] * NMOM
    far = [zero] * NMOM
    for s in range(SLICES):
        for row in range(ROWS):
            at = (s * ROWS + row) * CHUNK + 12
            test_near = mine_ref[at : at + 8, :]
            test_far = other_ref[at : at + 8, :]
            for order in range(NMOM):
                value = final_ref[order * ROWS + row, s : s + 1, :]
                near[order] = near[order] + test_near * value
                far[order] = far[order] + test_far * value
    stack = []
    for order in range(NMOM):
        stack.append(jnp.where(half == 0, near[order], far[order]))
        stack.append(jnp.where(half == 0, far[order], near[order]))
    sums = lax.dot_general(
        jnp.full((8, CELLS), scale, jnp.float32),
        jnp.concatenate(stack, axis=0),
        (((1,), (1,)), ((), ())),
        precision=HIGHEST,
        preferred_element_type=jnp.float32,
    )
    line = jnp.concatenate([sums, jnp.zeros_like(sums)], axis=1)[0:1]
    out_ref[pl.ds(2, DEVICES, stride=BACK), :] = jnp.broadcast_to(line, (DEVICES, CELLS))


def gather_kernel(blocks_ref, fields_ref, projected_ref):
    total = None
    for band in range(BANDS):
        first = band * PROBES * BACK
        for order in range(2):
            fields_ref[order, 0, band * PROBES : (band + 1) * PROBES, :] = blocks_ref[
                pl.ds(first + order, PROBES, stride=BACK), :
            ]
        part = blocks_ref[pl.ds(first + 2, PROBES, stride=BACK), :]
        total = part if total is None else total + part
    turned = total.T
    for order in range(2):
        fields_ref[order, 1] = jnp.zeros((BANDS * PROBES, CELLS), jnp.float32)
    for order in range(NMOM):
        projected_ref[order, 0] = turned[order * PROBES : (order + 1) * PROBES, :]
        projected_ref[order, 1] = jnp.zeros((PROBES, PROBES), jnp.float32)


FREQS = (0, SLICES // 2) + tuple(f for f in range(1, SLICES // 2) for _ in range(2))


def transform():
    s = np.arange(SLICES)
    rows = [np.cos(2 * np.pi * freq * s / SLICES) / np.sqrt(SLICES) for freq in FREQS[:2]]
    for freq in FREQS[2::2]:
        rows.append(np.sqrt(2.0 / SLICES) * np.cos(2 * np.pi * freq * s / SLICES))
        rows.append(np.sqrt(2.0 / SLICES) * np.sin(2 * np.pi * freq * s / SLICES))
    return np.array(rows)


def split_constant(matrix):
    matrix = matrix.astype(np.float32)
    high = matrix.astype(jnp.bfloat16)
    low = (matrix - high.astype(np.float32)).astype(jnp.bfloat16)
    return jnp.asarray(np.concatenate([high, high, low], axis=1))


def constants():
    wave = transform()
    cosine = np.array([math.cos(2 * math.pi * freq / SLICES) for freq in FREQS])
    spread = np.repeat(wave.T, BANDS, axis=1)
    return (
        [float(c) for c in cosine],
        split_constant(np.kron(wave, np.eye(BANDS))),
        jnp.asarray(spread, jnp.float32),
        jnp.asarray(np.repeat(cosine[:, None], CELLS, axis=1), jnp.float32),
        split_constant(wave),
        split_constant(wave.T),
    )


def contour():
    angles = [math.pi * (2 * point + 1) / PTS for point in range(HALF)]
    table = [[math.cos(a) for a in angles], [math.sin(a) for a in angles]]
    for function in (math.cos, math.sin):
        for order in range(NMOM):
            table.append([2.0 / PTS * function((order + 1) * a) for a in angles])
    return table


def vmem():
    return pl.BlockSpec(memory_space=pltpu.VMEM)


def smem():
    return pl.BlockSpec(memory_space=pltpu.SMEM)


def shape(*dims):
    return jax.ShapeDtypeStruct(dims, jnp.float32)


def params():
    return pltpu.CompilerParams(vmem_limit_bytes=VMEM_BYTES)


def exchange(blocks, rows, group):
    wide = blocks.reshape(DEVICES * rows // group, group, CELLS)
    if group > 1:
        wide = wide.reshape(DEVICES, rows // group, group, CELLS)
    wide = lax.all_to_all(wide, ALL, split_axis=0, concat_axis=0, tiled=True)
    return wide.reshape(DEVICES * rows, CELLS)


def on_device(
    probes, test_block, band_edge, slice_hop, cross_hop, deform, strain_elastic, strain_ids
):
    cut_count = lax.axis_size("cuts")
    raw = pl.BlockSpec(memory_space=pltpu.HBM)
    far = lambda x: pltpu.with_memory_space_constraint(x, pltpu.HBM)
    outgoing = pl.pallas_call(
        pack_kernel,
        out_shape=shape(DEVICES * CHUNK, CELLS),
        in_specs=[raw] * 4,
        out_specs=vmem(),
        scratch_shapes=[
            pltpu.VMEM((BANDS * PROBES, CELLS), jnp.float32),
            pltpu.VMEM((BANDS * PROBES, CELLS), jnp.float32),
            pltpu.VMEM((STRAINS, ROWS, CELLS // ROWS), jnp.float32),
            pltpu.VMEM((BANDS, CELLS), jnp.float32),
            pltpu.SemaphoreType.DMA((4,)),
        ],
        compiler_params=params(),
        name="pack",
    )(
        far(probes.reshape(BANDS * PROBES, CELLS)),
        far(test_block.reshape(BANDS * PROBES, CELLS)),
        far(jnp.transpose(strain_elastic[0], (1, 0, 2))),
        far(band_edge.reshape(BANDS, CELLS)),
    )
    mine = exchange(outgoing, CHUNK, 4)
    other = lax.ppermute(mine, "cuts", [(i, i ^ 1) for i in range(cut_count)])
    scale = (cut_count * BANDS * ROWS * CELLS) ** (-0.5)
    cosines, wave, spread, cosine, forth, back = constants()
    table = contour()
    high = lambda *dims: jax.ShapeDtypeStruct(dims, jnp.bfloat16)
    prepared = pl.pallas_call(
        prepare_kernel,
        out_shape=(
            high(TERMS * SLICES, 3 * SLICES * BANDS),
            shape(ROWS, SLICES * BANDS, CELLS),
            shape(BANDS, CELLS),
            shape(SLICES, CELLS),
        ),
        in_specs=[smem()] * 3 + [vmem()] * 4,
        out_specs=(vmem(),) * 4,
        scratch_shapes=[pltpu.VMEM((3 * SLICES * BANDS, PLANE), jnp.bfloat16)],
        compiler_params=params(),
        name="prepare",
    )(slice_hop, cross_hop, deform, mine, wave, spread, cosine)

    def main(*refs):
        main_kernel(scale, cosines, table, *refs)

    blocks = pl.pallas_call(
        main,
        out_shape=shape(DEVICES * BACK, CELLS),
        in_specs=[smem()] + [vmem()] * 8,
        out_specs=vmem(),
        scratch_shapes=[
            pltpu.SMEM((NSUB,), jnp.int32),
            pltpu.VMEM((ROWS, STRAINS * SLICES, CELLS), jnp.float32),
            pltpu.VMEM((STRAINS * SLICES, PLANE), jnp.float32),
            pltpu.VMEM((3 * SLICES * BANDS, 2 * PLANE), jnp.bfloat16),
            pltpu.VMEM((TERMS * SLICES, 2 * PLANE), jnp.float32),
            pltpu.VMEM((3 * SLICES, NMOM * PLANE), jnp.bfloat16),
            pltpu.VMEM((SLICES, NMOM * PLANE), jnp.float32),
            pltpu.VMEM((NMOM * ROWS, SLICES, CELLS), jnp.float32),
        ],
        compiler_params=params(),
        name="solve",
    )(strain_ids, mine, other, *prepared, forth, back)
    fields, projected = pl.pallas_call(
        gather_kernel,
        out_shape=(shape(2, 2, BANDS * PROBES, CELLS), shape(NMOM, 2, PROBES, PROBES)),
        in_specs=[vmem()],
        out_specs=(vmem(), vmem()),
        compiler_params=params(),
        name="gather",
    )(exchange(blocks, BACK, 1))
    return fields.reshape(2, 2, 1, BANDS, PROBES, 1, CELLS), projected


def solution(mesh):
    placed = (
        P("cuts", None, None, "tile", None),
        P("cuts", None, None, "tile", None),
        P(None, "tile", None),
        P(),
        P(),
        P(),
        P("cuts", "tile", None, None),
        P(),
    )
    return jax.shard_map(
        on_device,
        mesh=mesh,
        in_specs=placed,
        out_specs=(P(None, None, "cuts", None, None, "tile", None), P()),
        check_vma=False,
    )
```

```python
import math

import jax
import jax.numpy as jnp
import numpy as np
from jax import lax
from jax.experimental import pallas as pl
from jax.experimental.pallas import tpu as pltpu
from jax.sharding import PartitionSpec as P

PTS = 8
NMOM = 4
HALF = PTS // 2
ALL = ("cuts", "tile")

BANDS = 8
CELLS = 128
ROWS = 4
SLICES = 32
PROBES = 16
STRAINS = 6
TERMS = STRAINS + 4
PLANE = ROWS * CELLS
DEVICES = SLICES * ROWS
CHUNK = 20
BACK = 3
NSUB = ROWS * ROWS
HIGHEST = lax.Precision.HIGHEST
VMEM_BYTES = 20 * 1024 * 1024
PASSES = 1


def pack_kernel(
    probes_hbm,
    test_hbm,
    strain_hbm,
    edge_hbm,
    out_ref,
    probes_ref,
    test_ref,
    strain_ref,
    edge_ref,
    done,
):
    pairs = (
        (probes_hbm, probes_ref),
        (test_hbm, test_ref),
        (strain_hbm, strain_ref),
        (edge_hbm, edge_ref),
    )
    copies = [pltpu.make_async_copy(*pair, done.at[i]) for i, pair in enumerate(pairs)]
    for copy in copies:
        copy.start()
    copies[0].wait()
    for probe in range(PROBES):
        column = probes_ref[pl.ds(probe, BANDS, stride=PROBES), :]
        for band in range(BANDS):
            at = (band * PROBES + probe) * CHUNK
            out_ref[at : at + 8, :] = column
    copies[1].wait()
    for probe in range(PROBES):
        for band in range(BANDS):
            at = (band * PROBES + probe) * CHUNK
            first = band * PROBES + 8 * (probe // 4 % 2)
            out_ref[at + 12 : at + 20, :] = test_ref[first : first + 8, :]
    copies[2].wait()
    copies[3].wait()
    piece = lax.axis_index("cuts") % BANDS
    edge = edge_ref[pl.ds(piece, 1), :]
    strain = jnp.concatenate([strain_ref[:, slot, :] for slot in range(ROWS)], axis=1)
    for half in range(2):
        shared = jnp.concatenate([strain[3 * half : 3 * half + 3], edge], axis=0)
        for probe in range(PROBES):
            if probe // 4 % 2 == half:
                for band in range(BANDS):
                    at = (band * PROBES + probe) * CHUNK
                    out_ref[at + 8 : at + 12, :] = shared


def split(value):
    high = value.astype(jnp.bfloat16)
    low = (value - high.astype(jnp.float32)).astype(jnp.bfloat16)
    return high, low


def matmul(left, right):
    return jnp.dot(left, right, preferred_element_type=jnp.float32)


def keep(ref, at, lanes, value):
    size = ref.shape[0] // PASSES
    rows = slice(at, at + value.shape[0])
    if PASSES == 1:
        ref[rows, lanes] = value.astype(jnp.bfloat16)
        return
    high, low = split(value)
    ref[rows, lanes] = high
    ref[at + size : at + size + value.shape[0], lanes] = low
    if PASSES == 3:
        ref[at + 2 * size : at + 2 * size + value.shape[0], lanes] = high


def prepare_kernel(
    cosines,
    hop_ref,
    cross_ref,
    deform_ref,
    mine_ref,
    wave_ref,
    spread_ref,
    cosine_ref,
    result_ref,
    own_ref,
    shift_ref,
    field_ref,
    weights_ref,
    waves_ref,
    right_ref,
    power_ref,
    value_ref,
):
    band = lax.axis_index("cuts") // 4

    for s in range(0, SLICES, 2):
        for row in range(ROWS):
            pair = [
                mine_ref[((s + i) * ROWS + row) * CHUNK : ((s + i) * ROWS + row) * CHUNK + 8, :]
                for i in range(2)
            ]
            high, low = split(jnp.concatenate(pair, axis=0))
            lanes = slice(row * CELLS, (row + 1) * CELLS)
            at = s * BANDS
            field_ref[at : at + 16, lanes] = high
            field_ref[256 + at : 272 + at, lanes] = low
            field_ref[512 + at : 528 + at, lanes] = high
    waves = matmul(wave_ref[...], field_ref[...])
    for row in range(ROWS):
        waves_ref[row] = waves[:, row * CELLS : (row + 1) * CELLS]
        own_ref[:, row * CELLS : (row + 1) * CELLS] = waves_ref[
            row, pl.ds(band, SLICES, stride=BANDS), :
        ]

    source_band = lax.broadcasted_iota(jnp.int32, (1, SLICES * BANDS), 1) % BANDS
    for term in range(TERMS):
        line = jnp.zeros((1, SLICES * BANDS), jnp.float32)
        for src in range(BANDS):
            if term < STRAINS:
                entry = 0.5 * (deform_ref[term, band, src] + deform_ref[term, src, band])
            else:
                axis = (term - STRAINS) // 2
                if (term - STRAINS) % 2 == 0:
                    entry = cross_ref[axis, band, src]
                else:
                    entry = cross_ref[axis, src, band]
            line = jnp.where(source_band == src, entry, line)
        high, low = split(spread_ref[...] * line)
        at = slice(term * SLICES, (term + 1) * SLICES)
        for i, part in enumerate((high, high, low)[:PASSES]):
            weights_ref[at, i * 256 : (i + 1) * 256] = part

    sub = lax.broadcasted_iota(jnp.int32, (BANDS, CELLS), 0)
    hop = jnp.full((BANDS, CELLS), 2.0 * hop_ref[0], jnp.float32)
    for b in range(1, BANDS):
        hop = jnp.where(sub == b, 2.0 * hop_ref[b], hop)
    shift_ref[...] = 2.0 * hop_ref[band] * cosine_ref[...]

    def fields(row, _):
        edge = mine_ref[pl.ds(row * CHUNK + 11, BANDS, stride=ROWS * CHUNK), :]
        for step in range(HALF):
            for pair in range(SLICES // 2):
                rows = slice(pair * 16, pair * 16 + 16)
                if step == 0:
                    parts = []
                    for wave in (2 * pair, 2 * pair + 1):
                        if parts and cosines[wave] == cosines[wave - 1]:
                            parts.append(parts[0])
                            continue
                        energy = edge - hop * cosines[wave]
                        eighth = energy * energy
                        eighth = eighth * eighth
                        eighth = eighth * eighth
                        parts.append((energy, 1.0 / (1.0 + eighth)))
                    energy = jnp.concatenate([parts[0][0], parts[1][0]], axis=0)
                    inverse = jnp.concatenate([parts[0][1], parts[1][1]], axis=0)
                    value = inverse * waves_ref[row, rows, :]
                    power_ref[rows, :] = energy
                else:
                    energy = power_ref[rows, :]
                    value = value_ref[rows, :]
                after = value * energy
                for part, kept in enumerate((value, after)):
                    at = (2 * step + part) * CELLS
                    keep(right_ref, pair * 16, slice(at, at + CELLS), kept)
                if step < HALF - 1:
                    value_ref[rows, :] = after * energy
            lanes = slice(2 * step * CELLS, (2 * step + 2) * CELLS)
            result_ref[row, :, lanes] = matmul(weights_ref[...], right_ref[:, lanes])
        return 0

    lax.fori_loop(0, ROWS, fields, 0)


def main_kernel(
    scale,
    ids_ref,
    mine_ref,
    other_ref,
    result_ref,
    own_ref,
    shift_ref,
    forth_ref,
    back_ref,
    out_ref,
    place_ref,
    slots_ref,
    strain_ref,
    source_ref,
    moment_ref,
    final_ref,
):
    half = lax.axis_index("cuts") % 2
    band = lax.axis_index("cuts") // 4
    lane = lax.broadcasted_iota(jnp.int32, (SLICES, CELLS), 1)

    for slot in range(NSUB):
        place_ref[ids_ref[slot]] = slot
    for holder in range(ROWS):
        for comp in range(3):
            rows = pl.ds(holder * CHUNK + 8 + comp, SLICES, stride=ROWS * CHUNK)
            a = mine_ref[rows, :]
            b = other_ref[rows, :]
            slots_ref[holder, comp * SLICES : (comp + 1) * SLICES, :] = jnp.where(half == 0, a, b)
            slots_ref[holder, (comp + 3) * SLICES : (comp + 4) * SLICES, :] = jnp.where(
                half == 0, b, a
            )
    group = lax.broadcasted_iota(jnp.int32, (STRAINS * SLICES, CELLS), 1) // (CELLS // ROWS)
    for row in range(ROWS):
        total = None
        for part in range(ROWS):
            slot = place_ref[row * ROWS + part]
            shift = ((part + ROWS - slot % ROWS) % ROWS) * (CELLS // ROWS)
            rolled = pltpu.roll(slots_ref[slot // ROWS], shift, 1)
            total = rolled if total is None else jnp.where(group == part, rolled, total)
        strain_ref[:, row * CELLS : (row + 1) * CELLS] = total

    for row in range(ROWS):
        strains = [
            strain_ref[comp * SLICES : (comp + 1) * SLICES, row * CELLS : (row + 1) * CELLS]
            for comp in range(STRAINS)
        ]
        for field in range(PTS):
            lanes = slice(field * CELLS, (field + 1) * CELLS)
            total = None
            for comp in range(STRAINS):
                rows = slice(comp * SLICES, (comp + 1) * SLICES)
                value = strains[comp] * result_ref[row, rows, lanes]
                total = value if total is None else total + value
            from_right = pltpu.roll(result_ref[row, 192:224, lanes], CELLS - 1, 1)
            from_left = pltpu.roll(result_ref[row, 224:256, lanes], 1, 1)
            total = total + jnp.where(lane < CELLS - 1, from_right, 0.0)
            total = total + jnp.where(lane > 0, from_left, 0.0)
            if row < ROWS - 1:
                total = total + result_ref[row + 1, 256:288, lanes]
            if row > 0:
                total = total + result_ref[row - 1, 288:320, lanes]
            high, low = split(total)
            source_ref[0:32, lanes] = high
            source_ref[32:64, lanes] = low
            source_ref[64:96, lanes] = high
        coupled = matmul(forth_ref[...], source_ref[:, 0 : PTS * CELLS])
        terms = [coupled[:, field * CELLS : (field + 1) * CELLS] for field in range(PTS)]

        edge = mine_ref[pl.ds((band * ROWS + row) * CHUNK + 11, 1), :]
        energy = edge - shift_ref[...]
        powers = [None, energy]
        for _ in range(2, PTS):
            powers.append(powers[-1] * energy)
        inverse = 1.0 / (1.0 + powers[4] * powers[4])
        own = own_ref[:, row * CELLS : (row + 1) * CELLS]
        upper = terms[3]
        for field in range(4, PTS):
            upper = upper * energy + terms[field]
        uppers = [None, None, None, upper]
        for order in (2, 1, 0):
            uppers[order] = uppers[order + 1] + powers[PTS - 1 - order] * terms[order]
        lower = None
        for order in range(NMOM):
            value = own - uppers[order]
            if order > 0:
                lower = terms[0] if order == 1 else lower * energy + terms[order - 1]
                value = lower + powers[order] * value
            lanes = slice(order * PLANE + row * CELLS, order * PLANE + (row + 1) * CELLS)
            moment_ref[:, lanes] = inverse * value

    high, low = split(moment_ref[...])
    source_ref[0:32, :] = high
    source_ref[32:64, :] = low
    source_ref[64:96, :] = high
    final = matmul(back_ref[...], source_ref[...])
    for order in range(NMOM):
        for row in range(ROWS):
            at = order * PLANE + row * CELLS
            value = final[:, at : at + CELLS]
            final_ref[order * ROWS + row] = value
            if order < 2:
                out_ref[pl.ds(row * BACK + order, SLICES, stride=ROWS * BACK), :] = value

    zero = jnp.zeros((8, CELLS), jnp.float32)
    near = [zero] * NMOM
    far = [zero] * NMOM
    for s in range(SLICES):
        for row in range(ROWS):
            at = (s * ROWS + row) * CHUNK + 12
            test_near = mine_ref[at : at + 8, :]
            test_far = other_ref[at : at + 8, :]
            for order in range(NMOM):
                value = final_ref[order * ROWS + row, s : s + 1, :]
                near[order] = near[order] + test_near * value
                far[order] = far[order] + test_far * value
    stack = []
    for order in range(NMOM):
        stack.append(jnp.where(half == 0, near[order], far[order]))
        stack.append(jnp.where(half == 0, far[order], near[order]))
    sums = lax.dot_general(
        jnp.full((8, CELLS), scale, jnp.float32),
        jnp.concatenate(stack, axis=0),
        (((1,), (1,)), ((), ())),
        precision=HIGHEST,
        preferred_element_type=jnp.float32,
    )
    line = jnp.concatenate([sums, jnp.zeros_like(sums)], axis=1)[0:1]
    out_ref[pl.ds(2, DEVICES, stride=BACK), :] = jnp.broadcast_to(line, (DEVICES, CELLS))


def gather_kernel(blocks_ref, fields_ref, projected_ref):
    total = None
    for band in range(BANDS):
        first = band * PROBES * BACK
        for order in range(2):
            fields_ref[order, 0, band * PROBES : (band + 1) * PROBES, :] = blocks_ref[
                pl.ds(first + order, PROBES, stride=BACK), :
            ]
        part = blocks_ref[pl.ds(first + 2, PROBES, stride=BACK), :]
        total = part if total is None else total + part
    turned = total.T
    for order in range(2):
        fields_ref[order, 1] = jnp.zeros((BANDS * PROBES, CELLS), jnp.float32)
    for order in range(NMOM):
        projected_ref[order, 0] = turned[order * PROBES : (order + 1) * PROBES, :]
        projected_ref[order, 1] = jnp.zeros((PROBES, PROBES), jnp.float32)


FREQS = (0, SLICES // 2) + tuple(f for f in range(1, SLICES // 2) for _ in range(2))


def transform():
    s = np.arange(SLICES)
    rows = [np.cos(2 * np.pi * freq * s / SLICES) / np.sqrt(SLICES) for freq in FREQS[:2]]
    for freq in FREQS[2::2]:
        rows.append(np.sqrt(2.0 / SLICES) * np.cos(2 * np.pi * freq * s / SLICES))
        rows.append(np.sqrt(2.0 / SLICES) * np.sin(2 * np.pi * freq * s / SLICES))
    return np.array(rows)


def split_constant(matrix):
    matrix = matrix.astype(np.float32)
    high = matrix.astype(jnp.bfloat16)
    low = (matrix - high.astype(np.float32)).astype(jnp.bfloat16)
    return jnp.asarray(np.concatenate([high, high, low], axis=1))


def constants():
    wave = transform()
    cosine = np.array([math.cos(2 * math.pi * freq / SLICES) for freq in FREQS])
    spread = np.repeat(wave.T, BANDS, axis=1)
    return (
        [float(c) for c in cosine],
        split_constant(np.kron(wave, np.eye(BANDS))),
        jnp.asarray(spread, jnp.float32),
        jnp.asarray(np.repeat(cosine[:, None], CELLS, axis=1), jnp.float32),
        split_constant(wave),
        split_constant(wave.T),
    )


def vmem():
    return pl.BlockSpec(memory_space=pltpu.VMEM)


def smem():
    return pl.BlockSpec(memory_space=pltpu.SMEM)


def shape(*dims):
    return jax.ShapeDtypeStruct(dims, jnp.float32)


def params():
    return pltpu.CompilerParams(vmem_limit_bytes=VMEM_BYTES)


def exchange(blocks, rows, group):
    wide = blocks.reshape(DEVICES * rows // group, group, CELLS)
    if group > 1:
        wide = wide.reshape(DEVICES, rows // group, group, CELLS)
    wide = lax.all_to_all(wide, ALL, split_axis=0, concat_axis=0, tiled=True)
    return wide.reshape(DEVICES * rows, CELLS)


def on_device(
    probes, test_block, band_edge, slice_hop, cross_hop, deform, strain_elastic, strain_ids
):
    cut_count = lax.axis_size("cuts")
    raw = pl.BlockSpec(memory_space=pltpu.HBM)
    far = lambda x: pltpu.with_memory_space_constraint(x, pltpu.HBM)
    outgoing = pl.pallas_call(
        pack_kernel,
        out_shape=shape(DEVICES * CHUNK, CELLS),
        in_specs=[raw] * 4,
        out_specs=vmem(),
        scratch_shapes=[
            pltpu.VMEM((BANDS * PROBES, CELLS), jnp.float32),
            pltpu.VMEM((BANDS * PROBES, CELLS), jnp.float32),
            pltpu.VMEM((STRAINS, ROWS, CELLS // ROWS), jnp.float32),
            pltpu.VMEM((BANDS, CELLS), jnp.float32),
            pltpu.SemaphoreType.DMA((4,)),
        ],
        compiler_params=params(),
        name="pack",
    )(
        far(probes.reshape(BANDS * PROBES, CELLS)),
        far(test_block.reshape(BANDS * PROBES, CELLS)),
        far(jnp.transpose(strain_elastic[0], (1, 0, 2))),
        far(band_edge.reshape(BANDS, CELLS)),
    )
    mine = exchange(outgoing, CHUNK, 4)
    other = lax.ppermute(mine, "cuts", [(i, i ^ 1) for i in range(cut_count)])
    scale = (cut_count * BANDS * ROWS * CELLS) ** (-0.5)
    cosines, wave, spread, cosine, forth, back = constants()
    wide = SLICES * BANDS

    def prepare(*refs):
        prepare_kernel(cosines, *refs)

    prepared = pl.pallas_call(
        prepare,
        out_shape=(
            shape(ROWS, TERMS * SLICES, PTS * CELLS),
            shape(SLICES, PLANE),
            shape(SLICES, CELLS),
        ),
        in_specs=[smem()] * 3 + [vmem()] * 4,
        out_specs=(vmem(),) * 3,
        scratch_shapes=[
            pltpu.VMEM((3 * wide, PLANE), jnp.bfloat16),
            pltpu.VMEM((TERMS * SLICES, PASSES * wide), jnp.bfloat16),
            pltpu.VMEM((ROWS, wide, CELLS), jnp.float32),
            pltpu.VMEM((PASSES * wide, PTS * CELLS), jnp.bfloat16),
            pltpu.VMEM((wide, CELLS), jnp.float32),
            pltpu.VMEM((wide, CELLS), jnp.float32),
        ],
        compiler_params=params(),
        name="prepare",
    )(slice_hop, cross_hop, deform, mine, wave, spread, cosine)

    def main(*refs):
        main_kernel(scale, *refs)

    blocks = pl.pallas_call(
        main,
        out_shape=shape(DEVICES * BACK, CELLS),
        in_specs=[smem()] + [vmem()] * 7,
        out_specs=vmem(),
        scratch_shapes=[
            pltpu.SMEM((NSUB,), jnp.int32),
            pltpu.VMEM((ROWS, STRAINS * SLICES, CELLS), jnp.float32),
            pltpu.VMEM((STRAINS * SLICES, PLANE), jnp.float32),
            pltpu.VMEM((3 * SLICES, NMOM * PLANE), jnp.bfloat16),
            pltpu.VMEM((SLICES, NMOM * PLANE), jnp.float32),
            pltpu.VMEM((NMOM * ROWS, SLICES, CELLS), jnp.float32),
        ],
        compiler_params=params(),
        name="solve",
    )(strain_ids, mine, other, *prepared, forth, back)
    fields, projected = pl.pallas_call(
        gather_kernel,
        out_shape=(shape(2, 2, BANDS * PROBES, CELLS), shape(NMOM, 2, PROBES, PROBES)),
        in_specs=[vmem()],
        out_specs=(vmem(), vmem()),
        compiler_params=params(),
        name="gather",
    )(exchange(blocks, BACK, 1))
    return fields.reshape(2, 2, 1, BANDS, PROBES, 1, CELLS), projected


def solution(mesh):
    placed = (
        P("cuts", None, None, "tile", None),
        P("cuts", None, None, "tile", None),
        P(None, "tile", None),
        P(),
        P(),
        P(),
        P("cuts", "tile", None, None),
        P(),
    )
    return jax.shard_map(
        on_device,
        mesh=mesh,
        in_specs=placed,
        out_specs=(P(None, None, "cuts", None, None, "tile", None), P()),
        check_vma=False,
    )
```

```python
import math

import jax
import jax.numpy as jnp
import numpy as np
from jax import lax
from jax.experimental import pallas as pl
from jax.experimental.pallas import tpu as pltpu
from jax.sharding import PartitionSpec as P

PTS = 8
NMOM = 4
HALF = PTS // 2
ALL = ("cuts", "tile")

BANDS = 8
CELLS = 128
ROWS = 4
SLICES = 32
PROBES = 16
STRAINS = 6
TERMS = STRAINS + 4
PLANE = ROWS * CELLS
DEVICES = SLICES * ROWS
CHUNK = 20
BACK = 3
NSUB = ROWS * ROWS
HIGHEST = lax.Precision.HIGHEST
VMEM_BYTES = 20 * 1024 * 1024
PASSES = 1


def pack_kernel(
    probes_hbm,
    test_hbm,
    strain_hbm,
    edge_hbm,
    out_ref,
    probes_ref,
    test_ref,
    strain_ref,
    edge_ref,
    done,
):
    pairs = (
        (probes_hbm, probes_ref),
        (test_hbm, test_ref),
        (strain_hbm, strain_ref),
        (edge_hbm, edge_ref),
    )
    copies = [pltpu.make_async_copy(*pair, done.at[i]) for i, pair in enumerate(pairs)]
    for copy in copies:
        copy.start()
    copies[0].wait()
    for probe in range(PROBES):
        column = probes_ref[pl.ds(probe, BANDS, stride=PROBES), :]
        for band in range(BANDS):
            at = (band * PROBES + probe) * CHUNK
            out_ref[at : at + 8, :] = column
    copies[1].wait()
    for probe in range(PROBES):
        for band in range(BANDS):
            at = (band * PROBES + probe) * CHUNK
            first = band * PROBES + 8 * (probe // 4 % 2)
            out_ref[at + 12 : at + 20, :] = test_ref[first : first + 8, :]
    copies[2].wait()
    copies[3].wait()
    piece = lax.axis_index("cuts") % BANDS
    edge = edge_ref[pl.ds(piece, 1), :]
    strain = jnp.concatenate([strain_ref[:, slot, :] for slot in range(ROWS)], axis=1)
    for half in range(2):
        shared = jnp.concatenate([strain[3 * half : 3 * half + 3], edge], axis=0)
        for probe in range(PROBES):
            if probe // 4 % 2 == half:
                for band in range(BANDS):
                    at = (band * PROBES + probe) * CHUNK
                    out_ref[at + 8 : at + 12, :] = shared


def split(value):
    high = value.astype(jnp.bfloat16)
    low = (value - high.astype(jnp.float32)).astype(jnp.bfloat16)
    return high, low


def matmul(left, right):
    return jnp.dot(left, right, preferred_element_type=jnp.float32)


def keep(ref, at, lanes, value):
    size = ref.shape[0] // PASSES
    rows = slice(at, at + value.shape[0])
    if PASSES == 1:
        ref[rows, lanes] = value.astype(jnp.bfloat16)
        return
    high, low = split(value)
    ref[rows, lanes] = high
    ref[at + size : at + size + value.shape[0], lanes] = low
    if PASSES == 3:
        ref[at + 2 * size : at + 2 * size + value.shape[0], lanes] = high


def prepare_kernel(
    cosines,
    hop_hbm,
    cross_hbm,
    deform_hbm,
    ids_hbm,
    mine_ref,
    wave_ref,
    spread_ref,
    cosine_ref,
    result_ref,
    hops_ref,
    own_ref,
    shift_ref,
    place_ref,
    hop_ref,
    cross_ref,
    deform_ref,
    ids_ref,
    done,
    field_ref,
    weights_ref,
    waves_ref,
    right_ref,
    power_ref,
    value_ref,
    across_ref,
):
    band = lax.axis_index("cuts") // 4
    pairs = (
        (hop_hbm, hop_ref),
        (cross_hbm, cross_ref),
        (deform_hbm, deform_ref),
        (ids_hbm, ids_ref),
    )
    copies = [pltpu.make_async_copy(*pair, done.at[i]) for i, pair in enumerate(pairs)]
    for copy in copies:
        copy.start()

    for s in range(0, SLICES, 2):
        for row in range(ROWS):
            pair = [
                mine_ref[((s + i) * ROWS + row) * CHUNK : ((s + i) * ROWS + row) * CHUNK + 8, :]
                for i in range(2)
            ]
            high, low = split(jnp.concatenate(pair, axis=0))
            lanes = slice(row * CELLS, (row + 1) * CELLS)
            at = s * BANDS
            field_ref[at : at + 16, lanes] = high
            field_ref[256 + at : 272 + at, lanes] = low
            field_ref[512 + at : 528 + at, lanes] = high
    waves = matmul(wave_ref[...], field_ref[...])
    for row in range(ROWS):
        waves_ref[row] = waves[:, row * CELLS : (row + 1) * CELLS]
        own_ref[:, row * CELLS : (row + 1) * CELLS] = waves_ref[
            row, pl.ds(band, SLICES, stride=BANDS), :
        ]

    for copy in copies:
        copy.wait()

    width = CELLS // ROWS
    slot_cell = lax.broadcasted_iota(jnp.int32, (width, PLANE), 0)
    cell = lax.broadcasted_iota(jnp.int32, (width, PLANE), 1)
    diagonal = jnp.where(cell % width == slot_cell, cell // width, -1)
    for slot in range(NSUB):
        match = jnp.where(diagonal == ids_ref[slot], 1.0, 0.0)
        place_ref[slot * width : (slot + 1) * width, :] = match.astype(jnp.bfloat16)

    source_band = lax.broadcasted_iota(jnp.int32, (1, SLICES * BANDS), 1) % BANDS
    for term in range(TERMS):
        line = jnp.zeros((1, SLICES * BANDS), jnp.float32)
        for src in range(BANDS):
            if term < STRAINS:
                entry = 0.5 * (deform_ref[term, band, src] + deform_ref[term, src, band])
            else:
                axis = (term - STRAINS) // 2
                if (term - STRAINS) % 2 == 0:
                    entry = cross_ref[axis, band, src]
                else:
                    entry = cross_ref[axis, src, band]
            line = jnp.where(source_band == src, entry, line)
        high, low = split(spread_ref[...] * line)
        at = slice(term * SLICES, (term + 1) * SLICES)
        for i, part in enumerate((high, high, low)[:PASSES]):
            weights_ref[at, i * 256 : (i + 1) * 256] = part

    sub = lax.broadcasted_iota(jnp.int32, (BANDS, CELLS), 0)
    hop = jnp.full((BANDS, CELLS), 2.0 * hop_ref[0], jnp.float32)
    for b in range(1, BANDS):
        hop = jnp.where(sub == b, 2.0 * hop_ref[b], hop)
    shift_ref[...] = 2.0 * hop_ref[band] * cosine_ref[...]

    lane = lax.broadcasted_iota(jnp.int32, (SLICES, CELLS), 1)

    def fields(row, _):
        edge = mine_ref[pl.ds(row * CHUNK + 11, BANDS, stride=ROWS * CHUNK), :]
        for step in range(HALF):
            for pair in range(SLICES // 2):
                rows = slice(pair * 16, pair * 16 + 16)
                if step == 0:
                    parts = []
                    for wave in (2 * pair, 2 * pair + 1):
                        if parts and cosines[wave] == cosines[wave - 1]:
                            parts.append(parts[0])
                            continue
                        energy = edge - hop * cosines[wave]
                        eighth = energy * energy
                        eighth = eighth * eighth
                        eighth = eighth * eighth
                        parts.append((energy, 1.0 / (1.0 + eighth)))
                    energy = jnp.concatenate([parts[0][0], parts[1][0]], axis=0)
                    inverse = jnp.concatenate([parts[0][1], parts[1][1]], axis=0)
                    value = inverse * waves_ref[row, rows, :]
                    power_ref[rows, :] = energy
                else:
                    energy = power_ref[rows, :]
                    value = value_ref[rows, :]
                after = value * energy
                for part, kept in enumerate((value, after)):
                    at = (2 * step + part) * CELLS
                    keep(right_ref, pair * 16, slice(at, at + CELLS), kept)
                if step < HALF - 1:
                    value_ref[rows, :] = after * energy
            lanes = slice(2 * step * CELLS, (2 * step + 2) * CELLS)
            product = matmul(weights_ref[...], right_ref[:, lanes])
            result_ref[row, :, lanes] = product[0:192]
            across_ref[row, :, lanes] = product[256:320]
            for part in range(2):
                own = slice(part * CELLS, (part + 1) * CELLS)
                from_right = pltpu.roll(product[192:224, own], CELLS - 1, 1)
                from_left = pltpu.roll(product[224:256, own], 1, 1)
                at = (2 * step + part) * CELLS
                hops_ref[row, :, at : at + CELLS] = jnp.where(
                    lane < CELLS - 1, from_right, 0.0
                ) + jnp.where(lane > 0, from_left, 0.0)
        return 0

    for row in range(ROWS):
        fields(row, 0)
    for row in range(ROWS):
        if row < ROWS - 1:
            hops_ref[row] += across_ref[row + 1, 0:32]
        if row > 0:
            hops_ref[row] += across_ref[row - 1, 32:64]


def main_kernel(
    scale,
    mine_ref,
    other_ref,
    result_ref,
    hops_ref,
    own_ref,
    shift_ref,
    place_ref,
    forth_ref,
    back_ref,
    out_ref,
    high_ref,
    low_ref,
    strain_ref,
    source_ref,
    moment_ref,
    final_ref,
):
    half = lax.axis_index("cuts") % 2
    band = lax.axis_index("cuts") // 4

    for holder in range(ROWS):
        lanes = slice(holder * CELLS, (holder + 1) * CELLS)
        for comp in range(3):
            rows = pl.ds(holder * CHUNK + 8 + comp, SLICES, stride=ROWS * CHUNK)
            a = mine_ref[rows, :]
            b = other_ref[rows, :]
            for at, value in ((comp, jnp.where(half == 0, a, b)), (comp + 3, jnp.where(half == 0, b, a))):
                high, low = split(value)
                high_ref[at * SLICES : (at + 1) * SLICES, lanes] = high
                low_ref[at * SLICES : (at + 1) * SLICES, lanes] = low
    strain_ref[...] = matmul(high_ref[...], place_ref[...]) + matmul(low_ref[...], place_ref[...])

    for row in range(ROWS):
        strains = [
            strain_ref[comp * SLICES : (comp + 1) * SLICES, row * CELLS : (row + 1) * CELLS]
            for comp in range(STRAINS)
        ]
        for field in range(PTS):
            lanes = slice(field * CELLS, (field + 1) * CELLS)
            total = hops_ref[row, :, lanes]
            for comp in range(STRAINS):
                rows = slice(comp * SLICES, (comp + 1) * SLICES)
                total = total + strains[comp] * result_ref[row, rows, lanes]
            high, low = split(total)
            source_ref[0:32, lanes] = high
            source_ref[32:64, lanes] = low
            source_ref[64:96, lanes] = high
        coupled = matmul(forth_ref[...], source_ref[:, 0 : PTS * CELLS])
        terms = [coupled[:, field * CELLS : (field + 1) * CELLS] for field in range(PTS)]

        edge = mine_ref[pl.ds((band * ROWS + row) * CHUNK + 11, 1), :]
        energy = edge - shift_ref[...]
        powers = [None, energy]
        for _ in range(2, PTS):
            powers.append(powers[-1] * energy)
        inverse = 1.0 / (1.0 + powers[4] * powers[4])
        own = own_ref[:, row * CELLS : (row + 1) * CELLS]
        upper = terms[3]
        for field in range(4, PTS):
            upper = upper * energy + terms[field]
        uppers = [None, None, None, upper]
        for order in (2, 1, 0):
            uppers[order] = uppers[order + 1] + powers[PTS - 1 - order] * terms[order]
        lower = None
        for order in range(NMOM):
            value = own - uppers[order]
            if order > 0:
                lower = terms[0] if order == 1 else lower * energy + terms[order - 1]
                value = lower + powers[order] * value
            lanes = slice(order * PLANE + row * CELLS, order * PLANE + (row + 1) * CELLS)
            moment_ref[:, lanes] = inverse * value

    high, low = split(moment_ref[...])
    source_ref[0:32, :] = high
    source_ref[32:64, :] = low
    source_ref[64:96, :] = high
    final = matmul(back_ref[...], source_ref[...])
    for order in range(NMOM):
        for row in range(ROWS):
            at = order * PLANE + row * CELLS
            value = final[:, at : at + CELLS]
            final_ref[order * ROWS + row] = value
            if order < 2:
                out_ref[pl.ds(row * BACK + order, SLICES, stride=ROWS * BACK), :] = value

    zero = jnp.zeros((8, CELLS), jnp.float32)
    near = [zero] * NMOM
    far = [zero] * NMOM
    for s in range(SLICES):
        for row in range(ROWS):
            at = (s * ROWS + row) * CHUNK + 12
            test_near = mine_ref[at : at + 8, :]
            test_far = other_ref[at : at + 8, :]
            for order in range(NMOM):
                value = final_ref[order * ROWS + row, s : s + 1, :]
                near[order] = near[order] + test_near * value
                far[order] = far[order] + test_far * value
    stack = []
    for order in range(NMOM):
        stack.append(jnp.where(half == 0, near[order], far[order]))
        stack.append(jnp.where(half == 0, far[order], near[order]))
    sums = lax.dot_general(
        jnp.full((8, CELLS), scale, jnp.float32),
        jnp.concatenate(stack, axis=0),
        (((1,), (1,)), ((), ())),
        precision=HIGHEST,
        preferred_element_type=jnp.float32,
    )
    line = jnp.concatenate([sums, jnp.zeros_like(sums)], axis=1)[0:1]
    out_ref[pl.ds(2, DEVICES, stride=BACK), :] = jnp.broadcast_to(line, (DEVICES, CELLS))


def gather_kernel(blocks_ref, fields_ref, projected_ref):
    total = None
    for band in range(BANDS):
        first = band * PROBES * BACK
        for order in range(2):
            fields_ref[order, 0, band * PROBES : (band + 1) * PROBES, :] = blocks_ref[
                pl.ds(first + order, PROBES, stride=BACK), :
            ]
        part = blocks_ref[pl.ds(first + 2, PROBES, stride=BACK), :]
        total = part if total is None else total + part
    turned = total.T
    for order in range(2):
        fields_ref[order, 1] = jnp.zeros((BANDS * PROBES, CELLS), jnp.float32)
    for order in range(NMOM):
        projected_ref[order, 0] = turned[order * PROBES : (order + 1) * PROBES, :]
        projected_ref[order, 1] = jnp.zeros((PROBES, PROBES), jnp.float32)


FREQS = (0, SLICES // 2) + tuple(f for f in range(1, SLICES // 2) for _ in range(2))


def transform():
    s = np.arange(SLICES)
    rows = [np.cos(2 * np.pi * freq * s / SLICES) / np.sqrt(SLICES) for freq in FREQS[:2]]
    for freq in FREQS[2::2]:
        rows.append(np.sqrt(2.0 / SLICES) * np.cos(2 * np.pi * freq * s / SLICES))
        rows.append(np.sqrt(2.0 / SLICES) * np.sin(2 * np.pi * freq * s / SLICES))
    return np.array(rows)


def split_constant(matrix):
    matrix = matrix.astype(np.float32)
    high = matrix.astype(jnp.bfloat16)
    low = (matrix - high.astype(np.float32)).astype(jnp.bfloat16)
    return jnp.asarray(np.concatenate([high, high, low], axis=1))


def constants():
    wave = transform()
    cosine = np.array([math.cos(2 * math.pi * freq / SLICES) for freq in FREQS])
    spread = np.repeat(wave.T, BANDS, axis=1)
    return (
        [float(c) for c in cosine],
        split_constant(np.kron(wave, np.eye(BANDS))),
        jnp.asarray(spread, jnp.float32),
        jnp.asarray(np.repeat(cosine[:, None], CELLS, axis=1), jnp.float32),
        split_constant(wave),
        split_constant(wave.T),
    )


def vmem():
    return pl.BlockSpec(memory_space=pltpu.VMEM)


def shape(*dims):
    return jax.ShapeDtypeStruct(dims, jnp.float32)


def params():
    return pltpu.CompilerParams(vmem_limit_bytes=VMEM_BYTES)


def exchange(blocks, rows, group):
    wide = blocks.reshape(DEVICES * rows // group, group, CELLS)
    if group > 1:
        wide = wide.reshape(DEVICES, rows // group, group, CELLS)
    wide = lax.all_to_all(wide, ALL, split_axis=0, concat_axis=0, tiled=True)
    return wide.reshape(DEVICES * rows, CELLS)


def on_device(
    probes, test_block, band_edge, slice_hop, cross_hop, deform, strain_elastic, strain_ids
):
    cut_count = lax.axis_size("cuts")
    raw = pl.BlockSpec(memory_space=pltpu.HBM)
    far = lambda x: pltpu.with_memory_space_constraint(x, pltpu.HBM)
    outgoing = pl.pallas_call(
        pack_kernel,
        out_shape=shape(DEVICES * CHUNK, CELLS),
        in_specs=[raw] * 4,
        out_specs=vmem(),
        scratch_shapes=[
            pltpu.VMEM((BANDS * PROBES, CELLS), jnp.float32),
            pltpu.VMEM((BANDS * PROBES, CELLS), jnp.float32),
            pltpu.VMEM((STRAINS, ROWS, CELLS // ROWS), jnp.float32),
            pltpu.VMEM((BANDS, CELLS), jnp.float32),
            pltpu.SemaphoreType.DMA((4,)),
        ],
        compiler_params=params(),
        name="pack",
    )(
        far(probes.reshape(BANDS * PROBES, CELLS)),
        far(test_block.reshape(BANDS * PROBES, CELLS)),
        far(jnp.transpose(strain_elastic[0], (1, 0, 2))),
        far(band_edge.reshape(BANDS, CELLS)),
    )
    mine = exchange(outgoing, CHUNK, 4)
    other = lax.ppermute(mine, "cuts", [(i, i ^ 1) for i in range(cut_count)])
    scale = (cut_count * BANDS * ROWS * CELLS) ** (-0.5)
    cosines, wave, spread, cosine, forth, back = constants()
    wide = SLICES * BANDS

    def prepare(*refs):
        prepare_kernel(cosines, *refs)

    prepared = pl.pallas_call(
        prepare,
        out_shape=(
            shape(ROWS, STRAINS * SLICES, PTS * CELLS),
            shape(ROWS, SLICES, PTS * CELLS),
            shape(SLICES, PLANE),
            shape(SLICES, CELLS),
            jax.ShapeDtypeStruct((PLANE, PLANE), jnp.bfloat16),
        ),
        in_specs=[raw] * 4 + [vmem()] * 4,
        out_specs=(vmem(),) * 5,
        scratch_shapes=[
            pltpu.SMEM(slice_hop.shape, jnp.float32),
            pltpu.SMEM(cross_hop.shape, jnp.float32),
            pltpu.SMEM(deform.shape, jnp.float32),
            pltpu.SMEM(strain_ids.shape, jnp.int32),
            pltpu.SemaphoreType.DMA((4,)),
            pltpu.VMEM((3 * wide, PLANE), jnp.bfloat16),
            pltpu.VMEM((TERMS * SLICES, PASSES * wide), jnp.bfloat16),
            pltpu.VMEM((ROWS, wide, CELLS), jnp.float32),
            pltpu.VMEM((PASSES * wide, PTS * CELLS), jnp.bfloat16),
            pltpu.VMEM((wide, CELLS), jnp.float32),
            pltpu.VMEM((wide, CELLS), jnp.float32),
            pltpu.VMEM((ROWS, 2 * SLICES, PTS * CELLS), jnp.float32),
        ],
        compiler_params=params(),
        name="prepare",
    )(*map(far, (slice_hop, cross_hop, deform, strain_ids)), mine, wave, spread, cosine)

    def main(*refs):
        main_kernel(scale, *refs)

    blocks = pl.pallas_call(
        main,
        out_shape=shape(DEVICES * BACK, CELLS),
        in_specs=[vmem()] * 9,
        out_specs=vmem(),
        scratch_shapes=[
            pltpu.VMEM((STRAINS * SLICES, PLANE), jnp.bfloat16),
            pltpu.VMEM((STRAINS * SLICES, PLANE), jnp.bfloat16),
            pltpu.VMEM((STRAINS * SLICES, PLANE), jnp.float32),
            pltpu.VMEM((3 * SLICES, NMOM * PLANE), jnp.bfloat16),
            pltpu.VMEM((SLICES, NMOM * PLANE), jnp.float32),
            pltpu.VMEM((NMOM * ROWS, SLICES, CELLS), jnp.float32),
        ],
        compiler_params=params(),
        name="solve",
    )(mine, other, *prepared, forth, back)
    fields, projected = pl.pallas_call(
        gather_kernel,
        out_shape=(shape(2, 2, BANDS * PROBES, CELLS), shape(NMOM, 2, PROBES, PROBES)),
        in_specs=[vmem()],
        out_specs=(vmem(), vmem()),
        compiler_params=params(),
        name="gather",
    )(exchange(blocks, BACK, 1))
    return fields.reshape(2, 2, 1, BANDS, PROBES, 1, CELLS), projected


def solution(mesh):
    placed = (
        P("cuts", None, None, "tile", None),
        P("cuts", None, None, "tile", None),
        P(None, "tile", None),
        P(),
        P(),
        P(),
        P("cuts", "tile", None, None),
        P(),
    )
    return jax.shard_map(
        on_device,
        mesh=mesh,
        in_specs=placed,
        out_specs=(P(None, None, "cuts", None, None, "tile", None), P()),
        check_vma=False,
    )
```

```python
import math

import jax
import jax.numpy as jnp
import numpy as np
from jax import lax
from jax.experimental import pallas as pl
from jax.experimental.pallas import tpu as pltpu
from jax.sharding import PartitionSpec as P

PTS = 8
NMOM = 4
HALF = PTS // 2
ALL = ("cuts", "tile")

BANDS = 8
CELLS = 128
ROWS = 4
SLICES = 32
PROBES = 16
STRAINS = 6
TERMS = STRAINS + 4
PLANE = ROWS * CELLS
DEVICES = SLICES * ROWS
CHUNK = 17
PART = CELLS // 2
TEST, SLOTS, EDGE, NEXT = 8, 12, 15, 16
BACK = 3
NSUB = ROWS * ROWS
HIGHEST = lax.Precision.HIGHEST
VMEM_BYTES = 20 * 1024 * 1024
PASSES = 1


def pack_kernel(
    probes_hbm,
    test_hbm,
    strain_hbm,
    edge_hbm,
    out_ref,
    probes_ref,
    test_ref,
    strain_ref,
    edge_ref,
    done,
):
    pairs = (
        (probes_hbm, probes_ref),
        (test_hbm, test_ref),
        (strain_hbm, strain_ref),
        (edge_hbm, edge_ref),
    )
    copies = [pltpu.make_async_copy(*pair, done.at[i]) for i, pair in enumerate(pairs)]
    for copy in copies:
        copy.start()
    lane = lax.broadcasted_iota(jnp.int32, (BANDS, CELLS), 1)

    def beside(first, second, side):
        here = lane[: first.shape[0]] < PART
        if side == 0:
            return jnp.where(here, first, pltpu.roll(second, PART, 1))
        return jnp.where(here, pltpu.roll(first, PART, 1), second)

    def start(band, side, k):
        return (band * PROBES + side * BANDS + k) * CHUNK

    copies[0].wait()
    turned = probes_ref[...].T
    for k in range(BANDS):
        first = probes_ref[pl.ds(k, BANDS, stride=PROBES), :]
        second = probes_ref[pl.ds(k + BANDS, BANDS, stride=PROBES), :]
        for side in range(2):
            columns = beside(first, second, side)
            outer = turned[PART - side : PART - side + 1, :]
            for band in range(BANDS):
                at = start(band, side, k)
                out_ref[at : at + BANDS, :] = columns
                out_ref[at + NEXT : at + NEXT + 1, :] = outer
    copies[1].wait()
    for band in range(BANDS):
        for side in range(2):
            columns = beside(
                test_ref[band * PROBES : band * PROBES + 8, :],
                test_ref[band * PROBES + 8 : band * PROBES + 16, :],
                side,
            )
            for k in range(BANDS):
                at = start(band, side, k) + TEST
                half = k // 4
                out_ref[at : at + 4, :] = columns[4 * half : 4 * half + 4]
    copies[2].wait()
    copies[3].wait()
    piece = lax.axis_index("cuts") % BANDS
    edge = edge_ref[pl.ds(piece, 1), :]
    strain = jnp.concatenate([strain_ref[:, slot, :] for slot in range(ROWS)], axis=1)
    for half in range(2):
        shared = jnp.concatenate([strain[3 * half : 3 * half + 3], edge], axis=0)
        for k in range(4 * half, 4 * half + 4):
            for band in range(BANDS):
                for side in range(2):
                    at = start(band, side, k) + SLOTS
                    out_ref[at : at + 4, :] = shared


def split(value):
    high = value.astype(jnp.bfloat16)
    low = (value - high.astype(jnp.float32)).astype(jnp.bfloat16)
    return high, low


def matmul(left, right):
    return jnp.dot(left, right, preferred_element_type=jnp.float32)


def keep(ref, at, lanes, value):
    size = ref.shape[0] // PASSES
    rows = slice(at, at + value.shape[0])
    if PASSES == 1:
        ref[rows, lanes] = value.astype(jnp.bfloat16)
        return
    high, low = split(value)
    ref[rows, lanes] = high
    ref[at + size : at + size + value.shape[0], lanes] = low
    if PASSES == 3:
        ref[at + 2 * size : at + 2 * size + value.shape[0], lanes] = high


def prepare_kernel(
    cosines,
    hop_hbm,
    cross_hbm,
    deform_hbm,
    ids_hbm,
    mine_ref,
    wave_ref,
    spread_ref,
    cosine_ref,
    forth_ref,
    result_ref,
    hops_ref,
    outer_ref,
    own_ref,
    energy_ref,
    place_ref,
    hop_ref,
    cross_ref,
    deform_ref,
    ids_ref,
    done,
    field_ref,
    weights_ref,
    waves_ref,
    right_ref,
    power_ref,
    value_ref,
    across_ref,
    line_ref,
    bound_ref,
):
    band = lax.axis_index("cuts") // 4
    side = lax.axis_index("cuts") // 2 % 2
    k = lax.axis_index("cuts") % 2 * 4 + lax.axis_index("tile")
    pairs = (
        (hop_hbm, hop_ref),
        (cross_hbm, cross_ref),
        (deform_hbm, deform_ref),
        (ids_hbm, ids_ref),
    )
    copies = [pltpu.make_async_copy(*pair, done.at[i]) for i, pair in enumerate(pairs)]
    for copy in copies:
        copy.start()

    for s in range(0, SLICES, 2):
        for row in range(ROWS):
            pair = [
                mine_ref[((s + i) * ROWS + row) * CHUNK : ((s + i) * ROWS + row) * CHUNK + 8, :]
                for i in range(2)
            ]
            high, low = split(jnp.concatenate(pair, axis=0))
            lanes = slice(row * CELLS, (row + 1) * CELLS)
            at = s * BANDS
            field_ref[at : at + 16, lanes] = high
            field_ref[256 + at : 272 + at, lanes] = low
            field_ref[512 + at : 528 + at, lanes] = high
    waves = matmul(wave_ref[...], field_ref[...])
    for row in range(ROWS):
        waves_ref[row] = waves[:, row * CELLS : (row + 1) * CELLS]
        own_ref[:, row * CELLS : (row + 1) * CELLS] = waves_ref[
            row, pl.ds(band, SLICES, stride=BANDS), :
        ]

    for copy in copies:
        copy.wait()

    width = CELLS // ROWS
    slot_cell = lax.broadcasted_iota(jnp.int32, (width, PLANE), 0)
    cell = lax.broadcasted_iota(jnp.int32, (width, PLANE), 1)
    cell = cell // CELLS * CELLS + side * PART + cell % PART
    diagonal = jnp.where(cell % width == slot_cell, cell // width, -1)
    for slot in range(NSUB):
        match = jnp.where(diagonal == ids_ref[slot], 1.0, 0.0)
        place_ref[slot * width : (slot + 1) * width, :] = match.astype(jnp.bfloat16)

    source_band = lax.broadcasted_iota(jnp.int32, (1, SLICES * BANDS), 1) % BANDS
    for term in range(TERMS):
        line = jnp.zeros((1, SLICES * BANDS), jnp.float32)
        for src in range(BANDS):
            if term < STRAINS:
                entry = 0.5 * (deform_ref[term, band, src] + deform_ref[term, src, band])
            else:
                axis = (term - STRAINS) // 2
                if (term - STRAINS) % 2 == 0:
                    entry = cross_ref[axis, band, src]
                else:
                    entry = cross_ref[axis, src, band]
            line = jnp.where(source_band == src, entry, line)
        high, low = split(spread_ref[...] * line)
        at = slice(term * SLICES, (term + 1) * SLICES)
        for i, part in enumerate((high, high, low)[:PASSES]):
            weights_ref[at, i * 256 : (i + 1) * 256] = part

    sub = lax.broadcasted_iota(jnp.int32, (BANDS, CELLS), 0)
    hop = jnp.full((BANDS, CELLS), 2.0 * hop_ref[0], jnp.float32)
    for b in range(1, BANDS):
        hop = jnp.where(sub == b, 2.0 * hop_ref[b], hop)
    lane = lax.broadcasted_iota(jnp.int32, (SLICES, CELLS), 1)

    near = lane[:BANDS] < PART
    owner = lane[:BANDS] // PROBES == sub
    outer_hop = jnp.sum(jnp.where(owner, hop, 0.0), axis=0, keepdims=True)
    shift = 2.0 * hop_ref[band] * cosine_ref[...]
    edges = []
    for row in range(ROWS):
        edge = mine_ref[pl.ds(row * CHUNK + EDGE, BANDS, stride=ROWS * CHUNK), :]
        turned = pltpu.roll(edge, PART, 1)
        first = jnp.where(side == 0, edge, turned)
        second = jnp.where(side == 0, turned, edge)
        line_ref[...] = jnp.where(near, first, second)
        edges.append(line_ref[...])
        energy_ref[row] = line_ref[pl.ds(band, 1), :] - shift
        beyond = jnp.where(lane[:BANDS] == PART - side, edge, 0.0)
        beyond = jnp.sum(beyond, axis=1, keepdims=True)
        beyond = jnp.sum(jnp.where(owner, beyond, 0.0), axis=0, keepdims=True)
        lanes = slice(row * CELLS, (row + 1) * CELLS)
        high, low = split(mine_ref[pl.ds(row * CHUNK + NEXT, SLICES, stride=ROWS * CHUNK), :])
        field_ref[0:32, lanes] = high
        field_ref[32:64, lanes] = low
        field_ref[64:96, lanes] = high
        value = matmul(forth_ref[...], field_ref[0:96, lanes])
        energy = beyond - outer_hop * cosine_ref[...]
        eighth = energy * energy
        eighth = eighth * eighth
        eighth = eighth * eighth
        value = value * (1.0 / (1.0 + eighth))
        for field in range(PTS):
            at = (row * PTS + field) * SLICES
            bound_ref[at : at + SLICES, :] = value.astype(jnp.bfloat16)
            value = value * energy
    sub_two = lax.broadcasted_iota(jnp.int32, (PROBES, CELLS), 0)
    lane_two = lax.broadcasted_iota(jnp.int32, (PROBES, CELLS), 1)
    target = jnp.where(side == 0, PART - 1, 0)
    hit = ((sub_two == k) & (lane_two == target)) | (
        (sub_two == k + BANDS) & (lane_two == target + PART)
    )
    picks = []
    for src in range(BANDS):
        entry = jnp.where(side == 0, cross_ref[0, band, src], cross_ref[0, src, band])
        picks.append(jnp.where(hit, entry, 0.0))
    picks = jnp.concatenate(picks, axis=0).astype(jnp.bfloat16)
    outer_ref[...] = matmul(bound_ref[...], picks)

    def fields(row, _):
        edge = edges[row]
        for step in range(HALF):
            for pair in range(SLICES // 2):
                rows = slice(pair * 16, pair * 16 + 16)
                if step == 0:
                    parts = []
                    for wave in (2 * pair, 2 * pair + 1):
                        if parts and cosines[wave] == cosines[wave - 1]:
                            parts.append(parts[0])
                            continue
                        energy = edge - hop * cosines[wave]
                        eighth = energy * energy
                        eighth = eighth * eighth
                        eighth = eighth * eighth
                        parts.append((energy, 1.0 / (1.0 + eighth)))
                    energy = jnp.concatenate([parts[0][0], parts[1][0]], axis=0)
                    inverse = jnp.concatenate([parts[0][1], parts[1][1]], axis=0)
                    value = inverse * waves_ref[row, rows, :]
                    power_ref[rows, :] = energy
                else:
                    energy = power_ref[rows, :]
                    value = value_ref[rows, :]
                after = value * energy
                for part, kept in enumerate((value, after)):
                    at = (2 * step + part) * CELLS
                    keep(right_ref, pair * 16, slice(at, at + CELLS), kept)
                if step < HALF - 1:
                    value_ref[rows, :] = after * energy
            lanes = slice(2 * step * CELLS, (2 * step + 2) * CELLS)
            product = matmul(weights_ref[...], right_ref[:, lanes])
            result_ref[row, :, lanes] = product[0:192]
            across_ref[row, :, lanes] = product[256:320]
            for part in range(2):
                own = slice(part * CELLS, (part + 1) * CELLS)
                from_right = pltpu.roll(product[192:224, own], CELLS - 1, 1)
                from_left = pltpu.roll(product[224:256, own], 1, 1)
                at = (2 * step + part) * CELLS
                hops_ref[row, :, at : at + CELLS] = jnp.where(
                    lane % PART < PART - 1, from_right, 0.0
                ) + jnp.where(lane % PART > 0, from_left, 0.0)
        return 0

    for row in range(ROWS):
        fields(row, 0)
    for row in range(ROWS):
        if row < ROWS - 1:
            hops_ref[row] += across_ref[row + 1, 0:32]
        if row > 0:
            hops_ref[row] += across_ref[row - 1, 32:64]


def main_kernel(
    scale,
    mine_ref,
    other_ref,
    result_ref,
    hops_ref,
    outer_ref,
    own_ref,
    energy_ref,
    place_ref,
    forth_ref,
    back_ref,
    out_ref,
    high_ref,
    low_ref,
    strain_ref,
    source_ref,
    moment_ref,
    final_ref,
    swap_ref,
):
    half = lax.axis_index("cuts") % 2

    for holder in range(ROWS):
        lanes = slice(holder * CELLS, (holder + 1) * CELLS)
        for comp in range(3):
            rows = pl.ds(holder * CHUNK + SLOTS + comp, SLICES, stride=ROWS * CHUNK)
            a = mine_ref[rows, :]
            b = other_ref[rows, :]
            for at, value in ((comp, jnp.where(half == 0, a, b)), (comp + 3, jnp.where(half == 0, b, a))):
                high, low = split(value)
                high_ref[at * SLICES : (at + 1) * SLICES, lanes] = high
                low_ref[at * SLICES : (at + 1) * SLICES, lanes] = low
    strain_ref[...] = matmul(high_ref[...], place_ref[...]) + matmul(low_ref[...], place_ref[...])

    for row in range(ROWS):
        strains = [
            strain_ref[comp * SLICES : (comp + 1) * SLICES, row * CELLS : (row + 1) * CELLS]
            for comp in range(STRAINS)
        ]
        for field in range(PTS):
            lanes = slice(field * CELLS, (field + 1) * CELLS)
            total = hops_ref[row, :, lanes]
            for comp in range(STRAINS):
                rows = slice(comp * SLICES, (comp + 1) * SLICES)
                total = total + strains[comp] * result_ref[row, rows, lanes]
            high, low = split(total)
            source_ref[0:32, lanes] = high
            source_ref[32:64, lanes] = low
            source_ref[64:96, lanes] = high
        coupled = matmul(forth_ref[...], source_ref[:, 0 : PTS * CELLS])
        terms = []
        for field in range(PTS):
            at = (row * PTS + field) * SLICES
            terms.append(
                coupled[:, field * CELLS : (field + 1) * CELLS] + outer_ref[at : at + SLICES, :]
            )

        energy = energy_ref[row]
        powers = [None, energy]
        for _ in range(2, PTS):
            powers.append(powers[-1] * energy)
        inverse = 1.0 / (1.0 + powers[4] * powers[4])
        own = own_ref[:, row * CELLS : (row + 1) * CELLS]
        upper = terms[3]
        for field in range(4, PTS):
            upper = upper * energy + terms[field]
        uppers = [None, None, None, upper]
        for order in (2, 1, 0):
            uppers[order] = uppers[order + 1] + powers[PTS - 1 - order] * terms[order]
        lower = None
        for order in range(NMOM):
            value = own - uppers[order]
            if order > 0:
                lower = terms[0] if order == 1 else lower * energy + terms[order - 1]
                value = lower + powers[order] * value
            lanes = slice(order * PLANE + row * CELLS, order * PLANE + (row + 1) * CELLS)
            moment_ref[:, lanes] = inverse * value

    high, low = split(moment_ref[...])
    source_ref[0:32, :] = high
    source_ref[32:64, :] = low
    source_ref[64:96, :] = high
    final = matmul(back_ref[...], source_ref[...])
    for order in range(NMOM):
        for row in range(ROWS):
            at = order * PLANE + row * CELLS
            value = final[:, at : at + CELLS]
            final_ref[order * ROWS + row] = value
            if order < 2:
                out_ref[pl.ds(row * BACK + order, SLICES, stride=ROWS * BACK), :] = value

    zero = jnp.zeros((8, CELLS), jnp.float32)
    straight = [zero] * NMOM
    swapped = [zero] * NMOM
    for row in range(ROWS):
        for order in range(NMOM):
            swap_ref[order * ROWS + row] = pltpu.roll(final_ref[order * ROWS + row], PART, 1)
    for s in range(SLICES):
        for row in range(ROWS):
            at = (s * ROWS + row) * CHUNK + TEST
            test = jnp.concatenate([mine_ref[at : at + 4, :], other_ref[at : at + 4, :]], axis=0)
            for order in range(NMOM):
                line = order * ROWS + row
                straight[order] = straight[order] + test * final_ref[line, s : s + 1, :]
                swapped[order] = swapped[order] + test * swap_ref[line, s : s + 1, :]
    stack = []
    for order in range(NMOM):
        for total in (straight[order], swapped[order]):
            turned = jnp.concatenate([total[4:8], total[0:4]], axis=0)
            stack.append(jnp.where(half == 0, total, turned))
    sub = lax.broadcasted_iota(jnp.int32, (8, CELLS), 0)
    lane = lax.broadcasted_iota(jnp.int32, (8, CELLS), 1)
    sums = lax.dot_general(
        jnp.where(lane // PART == sub, jnp.float32(scale), 0.0),
        jnp.concatenate(stack, axis=0),
        (((1,), (1,)), ((), ())),
        precision=HIGHEST,
        preferred_element_type=jnp.float32,
    )
    line = jnp.concatenate([sums[0:1], sums[1:2]], axis=1)
    out_ref[pl.ds(2, DEVICES, stride=BACK), :] = jnp.broadcast_to(line, (DEVICES, CELLS))


def gather_kernel(blocks_ref, fields_ref, projected_ref):
    near = lax.broadcasted_iota(jnp.int32, (BANDS, CELLS), 1) < PART
    total = None
    for band in range(BANDS):
        for order in range(3):
            sides = [
                blocks_ref[
                    pl.ds((band * PROBES + side * BANDS) * BACK + order, BANDS, stride=BACK), :
                ]
                for side in range(2)
            ]
            if order == 2:
                part = sides[0] + sides[1]
                total = part if total is None else total + part
                continue
            at = band * PROBES
            fields_ref[order, 0, at : at + 8, :] = jnp.where(
                near, sides[0], pltpu.roll(sides[1], PART, 1)
            )
            fields_ref[order, 0, at + 8 : at + 16, :] = jnp.where(
                near, pltpu.roll(sides[0], PART, 1), sides[1]
            )
    for order in range(2):
        fields_ref[order, 1] = jnp.zeros((BANDS * PROBES, CELLS), jnp.float32)
    turned = total.T
    for order in range(NMOM):
        at = order * PROBES
        projected_ref[order, 0, 0:8, 0:8] = turned[at : at + 8, :]
        projected_ref[order, 0, 0:8, 8:16] = turned[at + 8 : at + 16, :]
        projected_ref[order, 0, 8:16, 0:8] = turned[PART + at + 8 : PART + at + 16, :]
        projected_ref[order, 0, 8:16, 8:16] = turned[PART + at : PART + at + 8, :]
        projected_ref[order, 1] = jnp.zeros((PROBES, PROBES), jnp.float32)


FREQS = (0, SLICES // 2) + tuple(f for f in range(1, SLICES // 2) for _ in range(2))


def transform():
    s = np.arange(SLICES)
    rows = [np.cos(2 * np.pi * freq * s / SLICES) / np.sqrt(SLICES) for freq in FREQS[:2]]
    for freq in FREQS[2::2]:
        rows.append(np.sqrt(2.0 / SLICES) * np.cos(2 * np.pi * freq * s / SLICES))
        rows.append(np.sqrt(2.0 / SLICES) * np.sin(2 * np.pi * freq * s / SLICES))
    return np.array(rows)


def split_constant(matrix):
    matrix = matrix.astype(np.float32)
    high = matrix.astype(jnp.bfloat16)
    low = (matrix - high.astype(np.float32)).astype(jnp.bfloat16)
    return jnp.asarray(np.concatenate([high, high, low], axis=1))


def constants():
    wave = transform()
    cosine = np.array([math.cos(2 * math.pi * freq / SLICES) for freq in FREQS])
    spread = np.repeat(wave.T, BANDS, axis=1)
    return (
        [float(c) for c in cosine],
        split_constant(np.kron(wave, np.eye(BANDS))),
        jnp.asarray(spread, jnp.float32),
        jnp.asarray(np.repeat(cosine[:, None], CELLS, axis=1), jnp.float32),
        split_constant(wave),
        split_constant(wave.T),
    )


def vmem():
    return pl.BlockSpec(memory_space=pltpu.VMEM)


def shape(*dims):
    return jax.ShapeDtypeStruct(dims, jnp.float32)


def params():
    return pltpu.CompilerParams(vmem_limit_bytes=VMEM_BYTES)


def exchange(blocks, rows):
    wide = blocks.reshape(DEVICES * rows, 1, CELLS)
    wide = lax.all_to_all(wide, ALL, split_axis=0, concat_axis=0, tiled=True)
    return wide.reshape(DEVICES * rows, CELLS)


def on_device(
    probes, test_block, band_edge, slice_hop, cross_hop, deform, strain_elastic, strain_ids
):
    cut_count = lax.axis_size("cuts")
    raw = pl.BlockSpec(memory_space=pltpu.HBM)
    far = lambda x: pltpu.with_memory_space_constraint(x, pltpu.HBM)
    outgoing = pl.pallas_call(
        pack_kernel,
        out_shape=shape(DEVICES * CHUNK, CELLS),
        in_specs=[raw] * 4,
        out_specs=vmem(),
        scratch_shapes=[
            pltpu.VMEM((BANDS * PROBES, CELLS), jnp.float32),
            pltpu.VMEM((BANDS * PROBES, CELLS), jnp.float32),
            pltpu.VMEM((STRAINS, ROWS, CELLS // ROWS), jnp.float32),
            pltpu.VMEM((BANDS, CELLS), jnp.float32),
            pltpu.SemaphoreType.DMA((4,)),
        ],
        compiler_params=params(),
        name="pack",
    )(
        far(probes.reshape(BANDS * PROBES, CELLS)),
        far(test_block.reshape(BANDS * PROBES, CELLS)),
        far(jnp.transpose(strain_elastic[0], (1, 0, 2))),
        far(band_edge.reshape(BANDS, CELLS)),
    )
    mine = exchange(outgoing, CHUNK)
    other = lax.ppermute(mine, "cuts", [(i, i ^ 1) for i in range(cut_count)])
    scale = (cut_count * BANDS * ROWS * CELLS) ** (-0.5)
    cosines, wave, spread, cosine, forth, back = constants()
    wide = SLICES * BANDS

    def prepare(*refs):
        prepare_kernel(cosines, *refs)

    prepared = pl.pallas_call(
        prepare,
        out_shape=(
            shape(ROWS, STRAINS * SLICES, PTS * CELLS),
            shape(ROWS, SLICES, PTS * CELLS),
            shape(ROWS * PTS * SLICES, CELLS),
            shape(SLICES, PLANE),
            shape(ROWS, SLICES, CELLS),
            jax.ShapeDtypeStruct((PLANE, PLANE), jnp.bfloat16),
        ),
        in_specs=[raw] * 4 + [vmem()] * 5,
        out_specs=(vmem(),) * 6,
        scratch_shapes=[
            pltpu.SMEM(slice_hop.shape, jnp.float32),
            pltpu.SMEM(cross_hop.shape, jnp.float32),
            pltpu.SMEM(deform.shape, jnp.float32),
            pltpu.SMEM(strain_ids.shape, jnp.int32),
            pltpu.SemaphoreType.DMA((4,)),
            pltpu.VMEM((3 * wide, PLANE), jnp.bfloat16),
            pltpu.VMEM((TERMS * SLICES, PASSES * wide), jnp.bfloat16),
            pltpu.VMEM((ROWS, wide, CELLS), jnp.float32),
            pltpu.VMEM((PASSES * wide, PTS * CELLS), jnp.bfloat16),
            pltpu.VMEM((wide, CELLS), jnp.float32),
            pltpu.VMEM((wide, CELLS), jnp.float32),
            pltpu.VMEM((ROWS, 2 * SLICES, PTS * CELLS), jnp.float32),
            pltpu.VMEM((BANDS, CELLS), jnp.float32),
            pltpu.VMEM((ROWS * PTS * SLICES, CELLS), jnp.bfloat16),
        ],
        compiler_params=params(),
        name="prepare",
    )(*map(far, (slice_hop, cross_hop, deform, strain_ids)), mine, wave, spread, cosine, forth)

    def main(*refs):
        main_kernel(scale, *refs)

    blocks = pl.pallas_call(
        main,
        out_shape=shape(DEVICES * BACK, CELLS),
        in_specs=[vmem()] * 10,
        out_specs=vmem(),
        scratch_shapes=[
            pltpu.VMEM((STRAINS * SLICES, PLANE), jnp.bfloat16),
            pltpu.VMEM((STRAINS * SLICES, PLANE), jnp.bfloat16),
            pltpu.VMEM((STRAINS * SLICES, PLANE), jnp.float32),
            pltpu.VMEM((3 * SLICES, NMOM * PLANE), jnp.bfloat16),
            pltpu.VMEM((SLICES, NMOM * PLANE), jnp.float32),
            pltpu.VMEM((NMOM * ROWS, SLICES, CELLS), jnp.float32),
            pltpu.VMEM((NMOM * ROWS, SLICES, CELLS), jnp.float32),
        ],
        compiler_params=params(),
        name="solve",
    )(mine, other, *prepared, forth, back)
    fields, projected = pl.pallas_call(
        gather_kernel,
        out_shape=(shape(2, 2, BANDS * PROBES, CELLS), shape(NMOM, 2, PROBES, PROBES)),
        in_specs=[vmem()],
        out_specs=(vmem(), vmem()),
        compiler_params=params(),
        name="gather",
    )(exchange(blocks, BACK))
    return fields.reshape(2, 2, 1, BANDS, PROBES, 1, CELLS), projected


def solution(mesh):
    placed = (
        P("cuts", None, None, "tile", None),
        P("cuts", None, None, "tile", None),
        P(None, "tile", None),
        P(),
        P(),
        P(),
        P("cuts", "tile", None, None),
        P(),
    )
    return jax.shard_map(
        on_device,
        mesh=mesh,
        in_specs=placed,
        out_specs=(P(None, None, "cuts", None, None, "tile", None), P()),
        check_vma=False,
    )
```

```python
import math

import jax
import jax.numpy as jnp
import numpy as np
from jax import lax
from jax.experimental import pallas as pl
from jax.experimental.pallas import tpu as pltpu
from jax.sharding import PartitionSpec as P

PTS = 8
NMOM = 4
HALF = PTS // 2
ALL = ("cuts", "tile")

BANDS = 8
CELLS = 128
ROWS = 4
SLICES = 32
PROBES = 16
STRAINS = 6
TERMS = STRAINS + 4
PLANE = ROWS * CELLS
DEVICES = SLICES * ROWS
CHUNK = 14
PARTS = 4
PART = CELLS // PARTS
TEST, SLOTS, EDGE = 8, 10, 13
OUTER, OUTER_EDGE = PART, 3 * PART
BACK = 4
NSUB = ROWS * ROWS
HIGHEST = lax.Precision.HIGHEST
PASSES = 1


def pack_kernel(
    probes_hbm,
    test_hbm,
    strain_hbm,
    edge_hbm,
    out_ref,
    probes_ref,
    test_ref,
    strain_ref,
    edge_ref,
    done,
):
    pairs = (
        (probes_hbm, probes_ref),
        (test_hbm, test_ref),
        (strain_hbm, strain_ref),
        (edge_hbm, edge_ref),
    )
    copies = [pltpu.make_async_copy(*pair, done.at[i]) for i, pair in enumerate(pairs)]
    for copy in copies:
        copy.start()
    lane = lax.broadcasted_iota(jnp.int32, (BANDS, CELLS), 1)

    def beside(parts, side):
        out = None
        for i, part in enumerate(parts):
            part = pltpu.roll(part, (i - side) * PART % CELLS, 1)
            here = lane[: part.shape[0]] // PART == i
            out = part if out is None else jnp.where(here, part, out)
        return out

    def start(band, side, k):
        return (band * PROBES + side // 2 * 8 + k * 2 + side % 2) * CHUNK

    copies[0].wait()
    stack = []
    for k in range(PARTS):
        parts = [
            probes_ref[pl.ds(k + PARTS * i, BANDS, stride=PROBES), :] for i in range(PARTS)
        ]
        stack += parts
        for side in range(PARTS):
            columns = beside(parts, side)
            for band in range(BANDS):
                at = start(band, side, k)
                out_ref[at : at + BANDS, :] = columns
    turned = jnp.concatenate(stack, axis=0).T
    line = lane[0:1]

    def bordering(k, side):
        total = jnp.zeros((1, CELLS), jnp.float32)
        for i, x in enumerate((side * PART - 1, (side + 1) * PART)):
            if 0 <= x < CELLS:
                at = OUTER + i * PART
                row = pltpu.roll(turned[x : x + 1, :], (at - PART * k) % CELLS, 1)
                total = jnp.where((line >= at) & (line < at + PART), row, total)
        return total

    copies[1].wait()
    for band in range(BANDS):
        first = band * PROBES
        parts = [test_ref[first + 4 * i : first + 4 * i + 4, :] for i in range(PARTS)]
        for side in range(PARTS):
            columns = beside(parts, side)
            for k in range(PARTS):
                at = start(band, side, k) + TEST
                half = k // 2
                out_ref[at : at + 2, :] = columns[2 * half : 2 * half + 2]
    copies[2].wait()
    copies[3].wait()
    piece = lax.axis_index("cuts") % BANDS
    edge = edge_ref[pl.ds(piece, 1), :]
    strain = jnp.concatenate([strain_ref[:, slot, :] for slot in range(ROWS)], axis=1)
    for side in range(PARTS):
        last = pltpu.roll(edge, -side * PART % CELLS, 1)
        last = jnp.where(line < PART, last, 0.0)
        for i, x in enumerate((side * PART - 1, (side + 1) * PART)):
            if 0 <= x < CELLS:
                beyond = jnp.where(line == x, edge, 0.0)
                beyond = jnp.sum(beyond, axis=1, keepdims=True)
                last = jnp.where(line == OUTER_EDGE + i, beyond, last)
        for k in range(PARTS):
            half = k // 2
            shared = jnp.concatenate([strain[3 * half : 3 * half + 3], last + bordering(k, side)])
            for band in range(BANDS):
                at = start(band, side, k) + SLOTS
                out_ref[at : at + 4, :] = shared


def split(value):
    high = value.astype(jnp.bfloat16)
    low = (value - high.astype(jnp.float32)).astype(jnp.bfloat16)
    return high, low


def matmul(left, right):
    return jnp.dot(left, right, preferred_element_type=jnp.float32)


def keep(ref, at, lanes, value):
    size = ref.shape[0] // PASSES
    rows = slice(at, at + value.shape[0])
    if PASSES == 1:
        ref[rows, lanes] = value.astype(jnp.bfloat16)
        return
    high, low = split(value)
    ref[rows, lanes] = high
    ref[at + size : at + size + value.shape[0], lanes] = low
    if PASSES == 3:
        ref[at + 2 * size : at + 2 * size + value.shape[0], lanes] = high


def prepare_kernel(
    cosines,
    hop_hbm,
    cross_hbm,
    deform_hbm,
    ids_hbm,
    spread_hbm,
    turns_hbm,
    mine_ref,
    wave_ref,
    result_ref,
    hops_ref,
    outer_ref,
    own_ref,
    energy_ref,
    place_ref,
    turns_ref,
    hop_ref,
    cross_ref,
    deform_ref,
    ids_ref,
    spread_ref,
    done,
    field_ref,
    weights_ref,
    waves_ref,
    right_ref,
    power_ref,
    value_ref,
    across_ref,
    line_ref,
    bound_ref,
):
    band = lax.axis_index("cuts") // 4
    side = lax.axis_index("cuts") // 2 % 2 * 2 + lax.axis_index("tile") % 2
    pairs = (
        (hop_hbm, hop_ref),
        (cross_hbm, cross_ref),
        (deform_hbm, deform_ref),
        (ids_hbm, ids_ref),
        (spread_hbm, spread_ref),
        (turns_hbm, turns_ref),
    )
    copies = [pltpu.make_async_copy(*pair, done.at[i]) for i, pair in enumerate(pairs)]
    for copy in copies:
        copy.start()

    for s in range(0, SLICES, 2):
        for row in range(ROWS):
            pair = [
                mine_ref[((s + i) * ROWS + row) * CHUNK : ((s + i) * ROWS + row) * CHUNK + 8, :]
                for i in range(2)
            ]
            high, low = split(jnp.concatenate(pair, axis=0))
            lanes = slice(row * CELLS, (row + 1) * CELLS)
            at = s * BANDS
            field_ref[at : at + 16, lanes] = high
            field_ref[256 + at : 272 + at, lanes] = low
            field_ref[512 + at : 528 + at, lanes] = high
    waves = matmul(wave_ref[...], field_ref[...])
    for row in range(ROWS):
        waves_ref[row] = waves[:, row * CELLS : (row + 1) * CELLS]
        own_ref[:, row * CELLS : (row + 1) * CELLS] = waves_ref[
            row, pl.ds(band, SLICES, stride=BANDS), :
        ]

    for copy in copies:
        copy.wait()

    width = CELLS // ROWS
    slot_cell = lax.broadcasted_iota(jnp.int32, (width, PLANE), 0)
    cell = lax.broadcasted_iota(jnp.int32, (width, PLANE), 1)
    cell = cell // CELLS * CELLS + side * PART + cell % PART
    diagonal = jnp.where(cell % width == slot_cell, cell // width, -1)
    for slot in range(NSUB):
        match = jnp.where(diagonal == ids_ref[slot], 1.0, 0.0)
        place_ref[slot * width : (slot + 1) * width, :] = match.astype(jnp.bfloat16)

    source_band = lax.broadcasted_iota(jnp.int32, (1, SLICES * BANDS), 1) % BANDS
    for term in range(TERMS):
        line = jnp.zeros((1, SLICES * BANDS), jnp.float32)
        for src in range(BANDS):
            if term < STRAINS:
                entry = 0.5 * (deform_ref[term, band, src] + deform_ref[term, src, band])
            else:
                axis = (term - STRAINS) // 2
                if (term - STRAINS) % 2 == 0:
                    entry = cross_ref[axis, band, src]
                else:
                    entry = cross_ref[axis, src, band]
            line = jnp.where(source_band == src, entry, line)
        high, low = split(spread_ref[:, 0:256] * line)
        at = slice(term * SLICES, (term + 1) * SLICES)
        for i, part in enumerate((high, high, low)[:PASSES]):
            weights_ref[at, i * 256 : (i + 1) * 256] = part

    sub = lax.broadcasted_iota(jnp.int32, (BANDS, CELLS), 0)
    hop = jnp.full((BANDS, CELLS), 2.0 * hop_ref[0], jnp.float32)
    for b in range(1, BANDS):
        hop = jnp.where(sub == b, 2.0 * hop_ref[b], hop)
    lane = lax.broadcasted_iota(jnp.int32, (SLICES, CELLS), 1)

    group = lane[:BANDS] // PART
    owner = (group >= 1) & (group < 3) & (lane[:BANDS] % BANDS == sub)
    outer_hop = jnp.sum(jnp.where(owner, hop, 0.0), axis=0, keepdims=True)
    cosine = spread_ref[:, 256:384]
    shift = 2.0 * hop_ref[band] * cosine
    edges = []
    for row in range(ROWS):
        edge = mine_ref[pl.ds(row * CHUNK + EDGE, BANDS, stride=ROWS * CHUNK), :]
        spread = edge
        for i in range(1, PARTS):
            spread = jnp.where(group == i, pltpu.roll(edge, i * PART, 1), spread)
        line_ref[...] = spread
        edges.append(spread)
        energy_ref[row] = line_ref[pl.ds(band, 1), :] - shift
        beyond = [
            jnp.sum(jnp.where(lane[:BANDS] == OUTER_EDGE + i, edge, 0.0), axis=1, keepdims=True)
            for i in range(2)
        ]
        beyond = jnp.where(group == 1, beyond[0], beyond[1])
        beyond = jnp.sum(jnp.where(owner, beyond, 0.0), axis=0, keepdims=True)
        lanes = slice(row * CELLS, (row + 1) * CELLS)
        high, low = split(mine_ref[pl.ds(row * CHUNK + EDGE, SLICES, stride=ROWS * CHUNK), :])
        field_ref[0:32, lanes] = high
        field_ref[32:64, lanes] = low
        field_ref[64:96, lanes] = high
        value = matmul(turns_ref[:, 0:96], field_ref[0:96, lanes])
        energy = beyond - outer_hop * cosine
        eighth = energy * energy
        eighth = eighth * eighth
        eighth = eighth * eighth
        value = value * (1.0 / (1.0 + eighth))
        for field in range(PTS):
            at = (row * PTS + field) * SLICES
            bound_ref[at : at + SLICES, :] = value.astype(jnp.bfloat16)
            value = value * energy
    sub_two = lax.broadcasted_iota(jnp.int32, (2 * PART, CELLS), 0)
    lane_two = lax.broadcasted_iota(jnp.int32, (2 * PART, CELLS), 1)
    entries = jnp.zeros((2 * PART, CELLS), jnp.float32)
    for src in range(BANDS):
        entry = jnp.where(sub_two < PART, cross_ref[0, src, band], cross_ref[0, band, src])
        entries = jnp.where(sub_two % BANDS == src, entry, entries)
    target = sub_two // BANDS % PARTS * PART + jnp.where(sub_two < PART, 0, PART - 1)
    picks = jnp.where(lane_two == target, entries, 0.0)
    rest = jnp.zeros((PART, CELLS), jnp.float32)
    picks = jnp.concatenate([rest, picks, rest], axis=0).astype(jnp.bfloat16)
    outer_ref[...] = matmul(bound_ref[...], picks)

    def fields(row, _):
        edge = edges[row]
        for step in range(HALF):
            for pair in range(SLICES // 2):
                rows = slice(pair * 16, pair * 16 + 16)
                if step == 0:
                    parts = []
                    for wave in (2 * pair, 2 * pair + 1):
                        if parts and cosines[wave] == cosines[wave - 1]:
                            parts.append(parts[0])
                            continue
                        energy = edge - hop * cosines[wave]
                        eighth = energy * energy
                        eighth = eighth * eighth
                        eighth = eighth * eighth
                        parts.append((energy, 1.0 / (1.0 + eighth)))
                    energy = jnp.concatenate([parts[0][0], parts[1][0]], axis=0)
                    inverse = jnp.concatenate([parts[0][1], parts[1][1]], axis=0)
                    value = inverse * waves_ref[row, rows, :]
                    power_ref[rows, :] = energy
                else:
                    energy = power_ref[rows, :]
                    value = value_ref[rows, :]
                after = value * energy
                for part, kept in enumerate((value, after)):
                    at = (2 * step + part) * CELLS
                    keep(right_ref, pair * 16, slice(at, at + CELLS), kept)
                if step < HALF - 1:
                    value_ref[rows, :] = after * energy
            lanes = slice(2 * step * CELLS, (2 * step + 2) * CELLS)
            product = matmul(weights_ref[...], right_ref[:, lanes])
            result_ref[row, :, lanes] = product[0:192]
            across_ref[row, :, lanes] = product[256:320]
            for part in range(2):
                own = slice(part * CELLS, (part + 1) * CELLS)
                from_right = pltpu.roll(product[192:224, own], CELLS - 1, 1)
                from_left = pltpu.roll(product[224:256, own], 1, 1)
                at = (2 * step + part) * CELLS
                hops_ref[row, :, at : at + CELLS] = jnp.where(
                    lane % PART < PART - 1, from_right, 0.0
                ) + jnp.where(lane % PART > 0, from_left, 0.0)
        return 0

    for row in range(ROWS):
        fields(row, 0)
    for row in range(ROWS):
        if row < ROWS - 1:
            hops_ref[row] += across_ref[row + 1, 0:32]
        if row > 0:
            hops_ref[row] += across_ref[row - 1, 32:64]


def main_kernel(
    scale,
    mine_ref,
    other_ref,
    result_ref,
    hops_ref,
    outer_ref,
    own_ref,
    energy_ref,
    place_ref,
    turns_ref,
    out_ref,
    high_ref,
    low_ref,
    strain_ref,
    source_ref,
    moment_ref,
    final_ref,
):
    half = lax.axis_index("cuts") % 2

    for holder in range(ROWS):
        lanes = slice(holder * CELLS, (holder + 1) * CELLS)
        for comp in range(3):
            rows = pl.ds(holder * CHUNK + SLOTS + comp, SLICES, stride=ROWS * CHUNK)
            a = mine_ref[rows, :]
            b = other_ref[rows, :]
            for at, value in ((comp, jnp.where(half == 0, a, b)), (comp + 3, jnp.where(half == 0, b, a))):
                high, low = split(value)
                high_ref[at * SLICES : (at + 1) * SLICES, lanes] = high
                low_ref[at * SLICES : (at + 1) * SLICES, lanes] = low
    strain_ref[...] = matmul(high_ref[...], place_ref[...]) + matmul(low_ref[...], place_ref[...])

    for row in range(ROWS):
        strains = [
            strain_ref[comp * SLICES : (comp + 1) * SLICES, row * CELLS : (row + 1) * CELLS]
            for comp in range(STRAINS)
        ]
        for field in range(PTS):
            lanes = slice(field * CELLS, (field + 1) * CELLS)
            total = hops_ref[row, :, lanes]
            for comp in range(STRAINS):
                rows = slice(comp * SLICES, (comp + 1) * SLICES)
                total = total + strains[comp] * result_ref[row, rows, lanes]
            high, low = split(total)
            source_ref[0:32, lanes] = high
            source_ref[32:64, lanes] = low
            source_ref[64:96, lanes] = high
        coupled = matmul(turns_ref[:, 0:96], source_ref[:, 0 : PTS * CELLS])
        terms = []
        for field in range(PTS):
            at = (row * PTS + field) * SLICES
            terms.append(
                coupled[:, field * CELLS : (field + 1) * CELLS] + outer_ref[at : at + SLICES, :]
            )

        energy = energy_ref[row]
        powers = [None, energy]
        for _ in range(2, PTS):
            powers.append(powers[-1] * energy)
        inverse = 1.0 / (1.0 + powers[4] * powers[4])
        own = own_ref[:, row * CELLS : (row + 1) * CELLS]
        upper = terms[3]
        for field in range(4, PTS):
            upper = upper * energy + terms[field]
        uppers = [None, None, None, upper]
        for order in (2, 1, 0):
            uppers[order] = uppers[order + 1] + powers[PTS - 1 - order] * terms[order]
        lower = None
        for order in range(NMOM):
            value = own - uppers[order]
            if order > 0:
                lower = terms[0] if order == 1 else lower * energy + terms[order - 1]
                value = lower + powers[order] * value
            lanes = slice(order * PLANE + row * CELLS, order * PLANE + (row + 1) * CELLS)
            moment_ref[:, lanes] = inverse * value

    high, low = split(moment_ref[...])
    source_ref[0:32, :] = high
    source_ref[32:64, :] = low
    source_ref[64:96, :] = high
    final = matmul(turns_ref[:, 96:192], source_ref[...])
    for order in range(NMOM):
        for row in range(ROWS):
            at = order * PLANE + row * CELLS
            value = final[:, at : at + CELLS]
            final_ref[order * ROWS + row] = value
            if order < 2:
                out_ref[pl.ds(row * BACK + order, SLICES, stride=ROWS * BACK), :] = value

    sub = lax.broadcasted_iota(jnp.int32, (8, CELLS), 0)
    lane = lax.broadcasted_iota(jnp.int32, (8, CELLS), 1)
    zero = jnp.zeros((8, CELLS), jnp.float32)
    totals = [[zero] * PARTS for _ in range(NMOM)]
    for s in range(SLICES):
        for row in range(0, ROWS, 2):
            parts = []
            for i in range(2):
                at = (s * ROWS + row + i) * CHUNK + TEST
                parts += [mine_ref[at : at + 2, :], other_ref[at : at + 2, :]]
            test = jnp.concatenate(parts, axis=0)
            tests = [test] + [pltpu.roll(test, i * PART, 1) for i in range(1, PARTS)]
            for order in range(NMOM):
                line = order * ROWS + row
                value = jnp.where(
                    sub < 4, final_ref[line, s : s + 1, :], final_ref[line + 1, s : s + 1, :]
                )
                for i in range(PARTS):
                    totals[order][i] = totals[order][i] + tests[i] * value
    stack = []
    for order in range(NMOM):
        for i in range(PARTS):
            total = totals[order][i][0:4] + totals[order][i][4:8]
            turned = jnp.concatenate([total[2:4], total[0:2]], axis=0)
            stack.append(jnp.where(half == 0, total, turned))
    sums = lax.dot_general(
        jnp.where(lane // PART == sub, jnp.float32(scale), 0.0),
        jnp.concatenate(stack, axis=0),
        (((1,), (1,)), ((), ())),
        precision=HIGHEST,
        preferred_element_type=jnp.float32,
    )
    for i in range(2):
        line = jnp.concatenate([sums[2 * i : 2 * i + 1], sums[2 * i + 1 : 2 * i + 2]], axis=1)
        out_ref[pl.ds(2 + i, DEVICES, stride=BACK), :] = jnp.broadcast_to(line, (DEVICES, CELLS))


def gather_kernel(blocks_ref, fields_ref, projected_ref):
    group = lax.broadcasted_iota(jnp.int32, (PROBES, CELLS), 1) // PART
    sums = [None, None]
    for band in range(BANDS):
        for order in range(4):
            sides = [
                blocks_ref[
                    pl.ds(
                        (band * PROBES + side // 2 * 8 + side % 2) * BACK + order,
                        PARTS,
                        stride=2 * BACK,
                    ),
                    :,
                ]
                for side in range(PARTS)
            ]
            if order >= 2:
                part = (sides[0] + sides[1]) + (sides[2] + sides[3])
                before = sums[order - 2]
                sums[order - 2] = part if before is None else before + part
                continue
            for i in range(PARTS):
                total = None
                for side in range(PARTS):
                    part = pltpu.roll(sides[side], (side - i) * PART % CELLS, 1)
                    total = part if total is None else jnp.where(group[:4] == side, part, total)
                at = band * PROBES + PARTS * i
                fields_ref[order, 0, at : at + PARTS, :] = total
    for order in range(2):
        fields_ref[order, 1] = jnp.zeros((BANDS * PROBES, CELLS), jnp.float32)
    turned = jnp.concatenate([sums[0], sums[1]], axis=0).T
    for order in range(NMOM):
        for probe in range(PARTS):
            first = probe % 2 * 64 + order * 16
            columns = slice(probe // 2 * PARTS, probe // 2 * PARTS + PARTS)
            for rotation in range(PARTS):
                test = (probe - rotation) % PARTS
                projected_ref[
                    order,
                    0,
                    PARTS * test : PARTS * test + PARTS,
                    PARTS * probe : PARTS * probe + PARTS,
                ] = turned[first + 4 * rotation : first + 4 * rotation + 4, columns]
        projected_ref[order, 1] = jnp.zeros((PROBES, PROBES), jnp.float32)


FREQS = (0, SLICES // 2) + tuple(f for f in range(1, SLICES // 2) for _ in range(2))


def transform():
    s = np.arange(SLICES)
    rows = [np.cos(2 * np.pi * freq * s / SLICES) / np.sqrt(SLICES) for freq in FREQS[:2]]
    for freq in FREQS[2::2]:
        rows.append(np.sqrt(2.0 / SLICES) * np.cos(2 * np.pi * freq * s / SLICES))
        rows.append(np.sqrt(2.0 / SLICES) * np.sin(2 * np.pi * freq * s / SLICES))
    return np.array(rows)


def split_constant(matrix):
    matrix = matrix.astype(np.float32)
    high = matrix.astype(jnp.bfloat16)
    low = (matrix - high.astype(np.float32)).astype(jnp.bfloat16)
    return jnp.asarray(np.concatenate([high, high, low], axis=1))


def constants():
    wave = transform()
    cosine = np.array([math.cos(2 * math.pi * freq / SLICES) for freq in FREQS])
    spread = np.repeat(wave.T, BANDS, axis=1)
    return (
        [float(c) for c in cosine],
        split_constant(np.kron(wave, np.eye(BANDS))),
        jnp.asarray(
            np.concatenate([spread, np.repeat(cosine[:, None], CELLS, axis=1)], axis=1),
            jnp.float32,
        ),
        jnp.concatenate([split_constant(wave), split_constant(wave.T)], axis=1),
    )


def vmem():
    return pl.BlockSpec(memory_space=pltpu.VMEM)


def shape(*dims):
    return jax.ShapeDtypeStruct(dims, jnp.float32)


def params(mebibytes):
    return pltpu.CompilerParams(vmem_limit_bytes=mebibytes * 1024 * 1024)


def exchange(blocks, rows):
    wide = blocks.reshape(DEVICES * rows, 1, CELLS)
    wide = lax.all_to_all(wide, ALL, split_axis=0, concat_axis=0, tiled=True)
    return wide.reshape(DEVICES * rows, CELLS)


def on_device(
    probes, test_block, band_edge, slice_hop, cross_hop, deform, strain_elastic, strain_ids
):
    cut_count = lax.axis_size("cuts")
    raw = pl.BlockSpec(memory_space=pltpu.HBM)
    far = lambda x: pltpu.with_memory_space_constraint(x, pltpu.HBM)
    outgoing = pl.pallas_call(
        pack_kernel,
        out_shape=shape(DEVICES * CHUNK, CELLS),
        in_specs=[raw] * 4,
        out_specs=vmem(),
        scratch_shapes=[
            pltpu.VMEM((BANDS * PROBES, CELLS), jnp.float32),
            pltpu.VMEM((BANDS * PROBES, CELLS), jnp.float32),
            pltpu.VMEM((STRAINS, ROWS, CELLS // ROWS), jnp.float32),
            pltpu.VMEM((BANDS, CELLS), jnp.float32),
            pltpu.SemaphoreType.DMA((4,)),
        ],
        compiler_params=params(8),
        name="pack",
    )(
        far(probes.reshape(BANDS * PROBES, CELLS)),
        far(test_block.reshape(BANDS * PROBES, CELLS)),
        far(jnp.transpose(strain_elastic[0], (1, 0, 2))),
        far(band_edge.reshape(BANDS, CELLS)),
    )
    mine = exchange(outgoing, CHUNK)
    other = lax.ppermute(mine, "cuts", [(i, i ^ 1) for i in range(cut_count)])
    scale = (cut_count * BANDS * ROWS * CELLS) ** (-0.5)
    cosines, wave, spread, turns = constants()
    wide = SLICES * BANDS

    def prepare(*refs):
        prepare_kernel(cosines, *refs)

    prepared = pl.pallas_call(
        prepare,
        out_shape=(
            shape(ROWS, STRAINS * SLICES, PTS * CELLS),
            shape(ROWS, SLICES, PTS * CELLS),
            shape(ROWS * PTS * SLICES, CELLS),
            shape(SLICES, PLANE),
            shape(ROWS, SLICES, CELLS),
            jax.ShapeDtypeStruct((PLANE, PLANE), jnp.bfloat16),
            jax.ShapeDtypeStruct(turns.shape, turns.dtype),
        ),
        in_specs=[raw] * 6 + [vmem()] * 2,
        out_specs=(vmem(),) * 7,
        scratch_shapes=[
            pltpu.SMEM(slice_hop.shape, jnp.float32),
            pltpu.SMEM(cross_hop.shape, jnp.float32),
            pltpu.SMEM(deform.shape, jnp.float32),
            pltpu.SMEM(strain_ids.shape, jnp.int32),
            pltpu.VMEM(spread.shape, jnp.float32),
            pltpu.SemaphoreType.DMA((6,)),
            pltpu.VMEM((3 * wide, PLANE), jnp.bfloat16),
            pltpu.VMEM((TERMS * SLICES, PASSES * wide), jnp.bfloat16),
            pltpu.VMEM((ROWS, wide, CELLS), jnp.float32),
            pltpu.VMEM((PASSES * wide, PTS * CELLS), jnp.bfloat16),
            pltpu.VMEM((wide, CELLS), jnp.float32),
            pltpu.VMEM((wide, CELLS), jnp.float32),
            pltpu.VMEM((ROWS, 2 * SLICES, PTS * CELLS), jnp.float32),
            pltpu.VMEM((BANDS, CELLS), jnp.float32),
            pltpu.VMEM((ROWS * PTS * SLICES, CELLS), jnp.bfloat16),
        ],
        compiler_params=params(20),
        name="prepare",
    )(
        *map(far, (slice_hop, cross_hop, deform, strain_ids, spread, turns)), mine, wave
    )

    def main(*refs):
        main_kernel(scale, *refs)

    blocks = pl.pallas_call(
        main,
        out_shape=shape(DEVICES * BACK, CELLS),
        in_specs=[vmem()] * 9,
        out_specs=vmem(),
        scratch_shapes=[
            pltpu.VMEM((STRAINS * SLICES, PLANE), jnp.bfloat16),
            pltpu.VMEM((STRAINS * SLICES, PLANE), jnp.bfloat16),
            pltpu.VMEM((STRAINS * SLICES, PLANE), jnp.float32),
            pltpu.VMEM((3 * SLICES, NMOM * PLANE), jnp.bfloat16),
            pltpu.VMEM((SLICES, NMOM * PLANE), jnp.float32),
            pltpu.VMEM((NMOM * ROWS, SLICES, CELLS), jnp.float32),
        ],
        compiler_params=params(20),
        name="solve",
    )(mine, other, *prepared)
    fields, projected = pl.pallas_call(
        gather_kernel,
        out_shape=(shape(2, 2, BANDS * PROBES, CELLS), shape(NMOM, 2, PROBES, PROBES)),
        in_specs=[vmem()],
        out_specs=(vmem(), vmem()),
        compiler_params=params(8),
        name="gather",
    )(exchange(blocks, BACK))
    return fields.reshape(2, 2, 1, BANDS, PROBES, 1, CELLS), projected


def solution(mesh):
    placed = (
        P("cuts", None, None, "tile", None),
        P("cuts", None, None, "tile", None),
        P(None, "tile", None),
        P(),
        P(),
        P(),
        P("cuts", "tile", None, None),
        P(),
    )
    return jax.shard_map(
        on_device,
        mesh=mesh,
        in_specs=placed,
        out_specs=(P(None, None, "cuts", None, None, "tile", None), P()),
        check_vma=False,
    )
```

```python
import math

import jax
import jax.numpy as jnp
import numpy as np
from jax import lax
from jax.experimental import pallas as pl
from jax.experimental.pallas import tpu as pltpu
from jax.sharding import PartitionSpec as P

PTS = 8
NMOM = 4
HALF = PTS // 2
ALL = ("cuts", "tile")

BANDS = 8
CELLS = 128
ROWS = 4
SLICES = 32
PROBES = 16
STRAINS = 6
TERMS = STRAINS + 4
PLANE = ROWS * CELLS
DEVICES = SLICES * ROWS
CHUNK = 14
PARTS = 4
PART = CELLS // PARTS
TEST, SLOTS, EDGE = 8, 10, 13
OUTER, OUTER_EDGE = PART, 3 * PART
BACK = 4
NSUB = ROWS * ROWS
HIGHEST = lax.Precision.HIGHEST
PASSES = 1


def pack_kernel(
    probes_hbm,
    test_hbm,
    strain_hbm,
    edge_hbm,
    out_ref,
    probes_ref,
    test_ref,
    strain_ref,
    edge_ref,
    done,
):
    pairs = (
        (probes_hbm, probes_ref),
        (test_hbm, test_ref),
        (strain_hbm, strain_ref),
        (edge_hbm, edge_ref),
    )
    copies = [pltpu.make_async_copy(*pair, done.at[i]) for i, pair in enumerate(pairs)]
    for copy in copies:
        copy.start()
    lane = lax.broadcasted_iota(jnp.int32, (BANDS, CELLS), 1)

    def beside(parts, side):
        out = None
        for i, part in enumerate(parts):
            part = pltpu.roll(part, (i - side) * PART % CELLS, 1)
            here = lane[: part.shape[0]] // PART == i
            out = part if out is None else jnp.where(here, part, out)
        return out

    def start(band, side, k):
        return (band * PROBES + side // 2 * 8 + k * 2 + side % 2) * CHUNK

    copies[0].wait()
    stack = []
    for k in range(PARTS):
        parts = [
            probes_ref[pl.ds(k + PARTS * i, BANDS, stride=PROBES), :] for i in range(PARTS)
        ]
        stack += parts
        for side in range(PARTS):
            columns = beside(parts, side)
            for band in range(BANDS):
                at = start(band, side, k)
                out_ref[at : at + BANDS, :] = columns
    turned = jnp.concatenate(stack, axis=0).T
    line = lane[0:1]

    def bordering(k, side):
        total = jnp.zeros((1, CELLS), jnp.float32)
        for i, x in enumerate((side * PART - 1, (side + 1) * PART)):
            if 0 <= x < CELLS:
                at = OUTER + i * PART
                row = pltpu.roll(turned[x : x + 1, :], (at - PART * k) % CELLS, 1)
                total = jnp.where((line >= at) & (line < at + PART), row, total)
        return total

    copies[1].wait()
    for band in range(BANDS):
        first = band * PROBES
        parts = [test_ref[first + 4 * i : first + 4 * i + 4, :] for i in range(PARTS)]
        for side in range(PARTS):
            columns = beside(parts, side)
            for k in range(PARTS):
                at = start(band, side, k) + TEST
                half = k // 2
                out_ref[at : at + 2, :] = columns[2 * half : 2 * half + 2]
    copies[2].wait()
    copies[3].wait()
    piece = lax.axis_index("cuts") % BANDS
    edge = edge_ref[pl.ds(piece, 1), :]
    strain = jnp.concatenate([strain_ref[:, slot, :] for slot in range(ROWS)], axis=1)
    for side in range(PARTS):
        last = pltpu.roll(edge, -side * PART % CELLS, 1)
        last = jnp.where(line < PART, last, 0.0)
        for i, x in enumerate((side * PART - 1, (side + 1) * PART)):
            if 0 <= x < CELLS:
                beyond = jnp.where(line == x, edge, 0.0)
                beyond = jnp.sum(beyond, axis=1, keepdims=True)
                last = jnp.where(line == OUTER_EDGE + i, beyond, last)
        for k in range(PARTS):
            half = k // 2
            shared = jnp.concatenate([strain[3 * half : 3 * half + 3], last + bordering(k, side)])
            for band in range(BANDS):
                at = start(band, side, k) + SLOTS
                out_ref[at : at + 4, :] = shared


def split(value):
    high = value.astype(jnp.bfloat16)
    low = (value - high.astype(jnp.float32)).astype(jnp.bfloat16)
    return high, low


def matmul(left, right):
    return jnp.dot(left, right, preferred_element_type=jnp.float32)


def keep(ref, at, lanes, value):
    size = ref.shape[0] // PASSES
    rows = slice(at, at + value.shape[0])
    if PASSES == 1:
        ref[rows, lanes] = value.astype(jnp.bfloat16)
        return
    high, low = split(value)
    ref[rows, lanes] = high
    ref[at + size : at + size + value.shape[0], lanes] = low
    if PASSES == 3:
        ref[at + 2 * size : at + 2 * size + value.shape[0], lanes] = high


def prepare_kernel(
    cosines,
    hop_hbm,
    cross_hbm,
    deform_hbm,
    ids_hbm,
    spread_hbm,
    turns_hbm,
    mine_ref,
    wave_ref,
    result_ref,
    hops_ref,
    outer_ref,
    own_ref,
    energy_ref,
    place_ref,
    turns_ref,
    hop_ref,
    cross_ref,
    deform_ref,
    ids_ref,
    spread_ref,
    done,
    field_ref,
    weights_ref,
    waves_ref,
    right_ref,
    power_ref,
    value_ref,
    across_ref,
    line_ref,
    bound_ref,
):
    band = lax.axis_index("cuts") // 4
    side = lax.axis_index("cuts") // 2 % 2 * 2 + lax.axis_index("tile") % 2
    pairs = (
        (hop_hbm, hop_ref),
        (cross_hbm, cross_ref),
        (deform_hbm, deform_ref),
        (ids_hbm, ids_ref),
        (spread_hbm, spread_ref),
        (turns_hbm, turns_ref),
    )
    copies = [pltpu.make_async_copy(*pair, done.at[i]) for i, pair in enumerate(pairs)]
    for copy in copies:
        copy.start()

    for s in range(0, SLICES, 2):
        for row in range(ROWS):
            pair = [
                mine_ref[((s + i) * ROWS + row) * CHUNK : ((s + i) * ROWS + row) * CHUNK + 8, :]
                for i in range(2)
            ]
            high, low = split(jnp.concatenate(pair, axis=0))
            lanes = slice(row * CELLS, (row + 1) * CELLS)
            at = s * BANDS
            field_ref[at : at + 16, lanes] = high
            field_ref[256 + at : 272 + at, lanes] = low
            field_ref[512 + at : 528 + at, lanes] = high
    for copy in copies:
        copy.wait()
    waves = matmul(wave_ref[...], field_ref[...])
    for row in range(ROWS):
        waves_ref[row] = waves[:, row * CELLS : (row + 1) * CELLS]
        own_ref[:, row * CELLS : (row + 1) * CELLS] = waves_ref[
            row, pl.ds(band, SLICES, stride=BANDS), :
        ]

    width = CELLS // ROWS
    slot_cell = lax.broadcasted_iota(jnp.int32, (width, PLANE), 0)
    cell = lax.broadcasted_iota(jnp.int32, (width, PLANE), 1)
    cell = cell // CELLS * CELLS + side * PART + cell % PART
    diagonal = jnp.where(cell % width == slot_cell, cell // width, -1)
    for slot in range(NSUB):
        match = jnp.where(diagonal == ids_ref[slot], 1.0, 0.0)
        place_ref[slot * width : (slot + 1) * width, :] = match.astype(jnp.bfloat16)

    source_band = lax.broadcasted_iota(jnp.int32, (1, SLICES * BANDS), 1) % BANDS
    for term in range(TERMS):
        line = jnp.zeros((1, SLICES * BANDS), jnp.float32)
        for src in range(BANDS):
            if term < STRAINS:
                entry = 0.5 * (deform_ref[term, band, src] + deform_ref[term, src, band])
            else:
                axis = (term - STRAINS) // 2
                if (term - STRAINS) % 2 == 0:
                    entry = cross_ref[axis, band, src]
                else:
                    entry = cross_ref[axis, src, band]
            line = jnp.where(source_band == src, entry, line)
        high, low = split(spread_ref[:, 0:256] * line)
        at = slice(term * SLICES, (term + 1) * SLICES)
        for i, part in enumerate((high, high, low)[:PASSES]):
            weights_ref[at, i * 256 : (i + 1) * 256] = part

    sub = lax.broadcasted_iota(jnp.int32, (BANDS, CELLS), 0)
    hop = jnp.full((BANDS, CELLS), 2.0 * hop_ref[0], jnp.float32)
    for b in range(1, BANDS):
        hop = jnp.where(sub == b, 2.0 * hop_ref[b], hop)
    lane = lax.broadcasted_iota(jnp.int32, (SLICES, CELLS), 1)

    group = lane[:BANDS] // PART
    owner = (group >= 1) & (group < 3) & (lane[:BANDS] % BANDS == sub)
    outer_hop = jnp.sum(jnp.where(owner, hop, 0.0), axis=0, keepdims=True)
    cosine = spread_ref[:, 256:384]
    shift = 2.0 * hop_ref[band] * cosine
    edges = []
    for row in range(ROWS):
        edge = mine_ref[pl.ds(row * CHUNK + EDGE, BANDS, stride=ROWS * CHUNK), :]
        spread = edge
        for i in range(1, PARTS):
            spread = jnp.where(group == i, pltpu.roll(edge, i * PART, 1), spread)
        line_ref[...] = spread
        edges.append(spread)
        energy_ref[row] = line_ref[pl.ds(band, 1), :] - shift
        beyond = [
            jnp.sum(jnp.where(lane[:BANDS] == OUTER_EDGE + i, edge, 0.0), axis=1, keepdims=True)
            for i in range(2)
        ]
        beyond = jnp.where(group == 1, beyond[0], beyond[1])
        beyond = jnp.sum(jnp.where(owner, beyond, 0.0), axis=0, keepdims=True)
        lanes = slice(row * CELLS, (row + 1) * CELLS)
        high, low = split(mine_ref[pl.ds(row * CHUNK + EDGE, SLICES, stride=ROWS * CHUNK), :])
        field_ref[0:32, lanes] = high
        field_ref[32:64, lanes] = low
        field_ref[64:96, lanes] = high
        value = matmul(turns_ref[:, 0:96], field_ref[0:96, lanes])
        energy = beyond - outer_hop * cosine
        eighth = energy * energy
        eighth = eighth * eighth
        eighth = eighth * eighth
        value = value * (1.0 / (1.0 + eighth))
        for field in range(PTS):
            at = (row * PTS + field) * SLICES
            bound_ref[at : at + SLICES, :] = value.astype(jnp.bfloat16)
            value = value * energy
    sub_two = lax.broadcasted_iota(jnp.int32, (2 * PART, CELLS), 0)
    lane_two = lax.broadcasted_iota(jnp.int32, (2 * PART, CELLS), 1)
    entries = jnp.zeros((2 * PART, CELLS), jnp.float32)
    for src in range(BANDS):
        entry = jnp.where(sub_two < PART, cross_ref[0, src, band], cross_ref[0, band, src])
        entries = jnp.where(sub_two % BANDS == src, entry, entries)
    target = sub_two // BANDS % PARTS * PART + jnp.where(sub_two < PART, 0, PART - 1)
    picks = jnp.where(lane_two == target, entries, 0.0)
    rest = jnp.zeros((PART, CELLS), jnp.float32)
    picks = jnp.concatenate([rest, picks, rest], axis=0).astype(jnp.bfloat16)
    outer_ref[...] = matmul(bound_ref[...], picks)

    def fields(row, _):
        edge = edges[row]
        for step in range(HALF):
            for pair in range(SLICES // 2):
                rows = slice(pair * 16, pair * 16 + 16)
                if step == 0:
                    parts = []
                    for wave in (2 * pair, 2 * pair + 1):
                        if parts and cosines[wave] == cosines[wave - 1]:
                            parts.append(parts[0])
                            continue
                        energy = edge - hop * cosines[wave]
                        eighth = energy * energy
                        eighth = eighth * eighth
                        eighth = eighth * eighth
                        parts.append((energy, 1.0 / (1.0 + eighth)))
                    energy = jnp.concatenate([parts[0][0], parts[1][0]], axis=0)
                    inverse = jnp.concatenate([parts[0][1], parts[1][1]], axis=0)
                    value = inverse * waves_ref[row, rows, :]
                    power_ref[rows, :] = energy
                else:
                    energy = power_ref[rows, :]
                    value = value_ref[rows, :]
                after = value * energy
                for part, kept in enumerate((value, after)):
                    at = (2 * step + part) * CELLS
                    keep(right_ref, pair * 16, slice(at, at + CELLS), kept)
                if step < HALF - 1:
                    value_ref[rows, :] = after * energy
            lanes = slice(2 * step * CELLS, (2 * step + 2) * CELLS)
            product = matmul(weights_ref[...], right_ref[:, lanes])
            result_ref[row, :, lanes] = product[0:192]
            across_ref[row, :, lanes] = product[256:320]
            for part in range(2):
                own = slice(part * CELLS, (part + 1) * CELLS)
                from_right = pltpu.roll(product[192:224, own], CELLS - 1, 1)
                from_left = pltpu.roll(product[224:256, own], 1, 1)
                at = (2 * step + part) * CELLS
                hops_ref[row, :, at : at + CELLS] = jnp.where(
                    lane % PART < PART - 1, from_right, 0.0
                ) + jnp.where(lane % PART > 0, from_left, 0.0)
        return 0

    for row in range(ROWS):
        fields(row, 0)
    for row in range(ROWS):
        if row < ROWS - 1:
            hops_ref[row] += across_ref[row + 1, 0:32]
        if row > 0:
            hops_ref[row] += across_ref[row - 1, 32:64]


def main_kernel(
    scale,
    mine_ref,
    other_ref,
    result_ref,
    hops_ref,
    outer_ref,
    own_ref,
    energy_ref,
    place_ref,
    turns_ref,
    out_ref,
    high_ref,
    low_ref,
    strain_ref,
    source_ref,
    moment_ref,
    final_ref,
):
    half = lax.axis_index("cuts") % 2

    for holder in range(ROWS):
        lanes = slice(holder * CELLS, (holder + 1) * CELLS)
        for comp in range(3):
            rows = pl.ds(holder * CHUNK + SLOTS + comp, SLICES, stride=ROWS * CHUNK)
            a = mine_ref[rows, :]
            b = other_ref[rows, :]
            for at, value in ((comp, jnp.where(half == 0, a, b)), (comp + 3, jnp.where(half == 0, b, a))):
                high, low = split(value)
                high_ref[at * SLICES : (at + 1) * SLICES, lanes] = high
                low_ref[at * SLICES : (at + 1) * SLICES, lanes] = low
    strain_ref[...] = matmul(high_ref[...], place_ref[...]) + matmul(low_ref[...], place_ref[...])

    for row in range(ROWS):
        strains = [
            strain_ref[comp * SLICES : (comp + 1) * SLICES, row * CELLS : (row + 1) * CELLS]
            for comp in range(STRAINS)
        ]
        for field in range(PTS):
            lanes = slice(field * CELLS, (field + 1) * CELLS)
            total = hops_ref[row, :, lanes]
            for comp in range(STRAINS):
                rows = slice(comp * SLICES, (comp + 1) * SLICES)
                total = total + strains[comp] * result_ref[row, rows, lanes]
            high, low = split(total)
            source_ref[0:32, lanes] = high
            source_ref[32:64, lanes] = low
            source_ref[64:96, lanes] = high
        coupled = matmul(turns_ref[:, 0:96], source_ref[:, 0 : PTS * CELLS])
        terms = []
        for field in range(PTS):
            at = (row * PTS + field) * SLICES
            terms.append(
                coupled[:, field * CELLS : (field + 1) * CELLS] + outer_ref[at : at + SLICES, :]
            )

        energy = energy_ref[row]
        powers = [None, energy]
        for _ in range(2, PTS):
            powers.append(powers[-1] * energy)
        inverse = 1.0 / (1.0 + powers[4] * powers[4])
        own = own_ref[:, row * CELLS : (row + 1) * CELLS]
        upper = terms[3]
        for field in range(4, PTS):
            upper = upper * energy + terms[field]
        uppers = [None, None, None, upper]
        for order in (2, 1, 0):
            uppers[order] = uppers[order + 1] + powers[PTS - 1 - order] * terms[order]
        lower = None
        for order in range(NMOM):
            value = own - uppers[order]
            if order > 0:
                lower = terms[0] if order == 1 else lower * energy + terms[order - 1]
                value = lower + powers[order] * value
            lanes = slice(order * PLANE + row * CELLS, order * PLANE + (row + 1) * CELLS)
            moment_ref[:, lanes] = inverse * value

    high, low = split(moment_ref[...])
    source_ref[0:32, :] = high
    source_ref[32:64, :] = low
    source_ref[64:96, :] = high
    final = matmul(turns_ref[:, 96:192], source_ref[...])
    for order in range(NMOM):
        for row in range(ROWS):
            at = order * PLANE + row * CELLS
            value = final[:, at : at + CELLS]
            final_ref[order * ROWS + row] = value
            if order < 2:
                out_ref[pl.ds(row * BACK + order, SLICES, stride=ROWS * BACK), :] = value

    sub = lax.broadcasted_iota(jnp.int32, (8, CELLS), 0)
    lane = lax.broadcasted_iota(jnp.int32, (8, CELLS), 1)
    zero = jnp.zeros((8, CELLS), jnp.float32)
    totals = [[zero] * PARTS for _ in range(NMOM)]
    for s in range(SLICES):
        for row in range(0, ROWS, 2):
            parts = []
            for i in range(2):
                at = (s * ROWS + row + i) * CHUNK + TEST
                parts += [mine_ref[at : at + 2, :], other_ref[at : at + 2, :]]
            test = jnp.concatenate(parts, axis=0)
            tests = [test] + [pltpu.roll(test, i * PART, 1) for i in range(1, PARTS)]
            for order in range(NMOM):
                line = order * ROWS + row
                value = jnp.where(
                    sub < 4, final_ref[line, s : s + 1, :], final_ref[line + 1, s : s + 1, :]
                )
                for i in range(PARTS):
                    totals[order][i] = totals[order][i] + tests[i] * value
    stack = []
    for order in range(NMOM):
        for i in range(PARTS):
            total = totals[order][i][0:4] + totals[order][i][4:8]
            turned = jnp.concatenate([total[2:4], total[0:2]], axis=0)
            stack.append(jnp.where(half == 0, total, turned))
    sums = lax.dot_general(
        jnp.where(lane // PART == sub, jnp.float32(scale), 0.0),
        jnp.concatenate(stack, axis=0),
        (((1,), (1,)), ((), ())),
        precision=HIGHEST,
        preferred_element_type=jnp.float32,
    )
    for i in range(2):
        line = jnp.concatenate([sums[2 * i : 2 * i + 1], sums[2 * i + 1 : 2 * i + 2]], axis=1)
        out_ref[pl.ds(2 + i, DEVICES, stride=BACK), :] = jnp.broadcast_to(line, (DEVICES, CELLS))


def gather_kernel(blocks_ref, fields_ref, projected_ref):
    group = lax.broadcasted_iota(jnp.int32, (PROBES, CELLS), 1) // PART
    sums = [None, None]
    for band in range(BANDS):
        for order in range(4):
            sides = [
                blocks_ref[
                    pl.ds(
                        (band * PROBES + side // 2 * 8 + side % 2) * BACK + order,
                        PARTS,
                        stride=2 * BACK,
                    ),
                    :,
                ]
                for side in range(PARTS)
            ]
            if order >= 2:
                part = (sides[0] + sides[1]) + (sides[2] + sides[3])
                before = sums[order - 2]
                sums[order - 2] = part if before is None else before + part
                continue
            for i in range(PARTS):
                total = None
                for side in range(PARTS):
                    part = pltpu.roll(sides[side], (side - i) * PART % CELLS, 1)
                    total = part if total is None else jnp.where(group[:4] == side, part, total)
                at = band * PROBES + PARTS * i
                fields_ref[order, 0, at : at + PARTS, :] = total
    for order in range(2):
        fields_ref[order, 1] = jnp.zeros((BANDS * PROBES, CELLS), jnp.float32)
    turned = jnp.concatenate([sums[0], sums[1]], axis=0).T
    for order in range(NMOM):
        for probe in range(PARTS):
            first = probe % 2 * 64 + order * 16
            columns = slice(probe // 2 * PARTS, probe // 2 * PARTS + PARTS)
            for rotation in range(PARTS):
                test = (probe - rotation) % PARTS
                projected_ref[
                    order,
                    0,
                    PARTS * test : PARTS * test + PARTS,
                    PARTS * probe : PARTS * probe + PARTS,
                ] = turned[first + 4 * rotation : first + 4 * rotation + 4, columns]
        projected_ref[order, 1] = jnp.zeros((PROBES, PROBES), jnp.float32)


FREQS = (0, SLICES // 2) + tuple(f for f in range(1, SLICES // 2) for _ in range(2))


def transform():
    s = np.arange(SLICES)
    rows = [np.cos(2 * np.pi * freq * s / SLICES) / np.sqrt(SLICES) for freq in FREQS[:2]]
    for freq in FREQS[2::2]:
        rows.append(np.sqrt(2.0 / SLICES) * np.cos(2 * np.pi * freq * s / SLICES))
        rows.append(np.sqrt(2.0 / SLICES) * np.sin(2 * np.pi * freq * s / SLICES))
    return np.array(rows)


def split_constant(matrix):
    matrix = matrix.astype(np.float32)
    high = matrix.astype(jnp.bfloat16)
    low = (matrix - high.astype(np.float32)).astype(jnp.bfloat16)
    return jnp.asarray(np.concatenate([high, high, low], axis=1))


def constants():
    wave = transform()
    cosine = np.array([math.cos(2 * math.pi * freq / SLICES) for freq in FREQS])
    spread = np.repeat(wave.T, BANDS, axis=1)
    return (
        [float(c) for c in cosine],
        split_constant(np.kron(wave, np.eye(BANDS))),
        jnp.asarray(
            np.concatenate([spread, np.repeat(cosine[:, None], CELLS, axis=1)], axis=1),
            jnp.float32,
        ),
        jnp.concatenate([split_constant(wave), split_constant(wave.T)], axis=1),
    )


def vmem():
    return pl.BlockSpec(memory_space=pltpu.VMEM)


def shape(*dims):
    return jax.ShapeDtypeStruct(dims, jnp.float32)


def params(mebibytes):
    return pltpu.CompilerParams(vmem_limit_bytes=mebibytes * 1024 * 1024)


def exchange(blocks, rows):
    wide = blocks.reshape(DEVICES * rows, 1, CELLS)
    wide = lax.all_to_all(wide, ALL, split_axis=0, concat_axis=0, tiled=True)
    return wide.reshape(DEVICES * rows, CELLS)


def on_device(
    probes, test_block, band_edge, slice_hop, cross_hop, deform, strain_elastic, strain_ids
):
    cut_count = lax.axis_size("cuts")
    raw = pl.BlockSpec(memory_space=pltpu.HBM)
    far = lambda x: pltpu.with_memory_space_constraint(x, pltpu.HBM)
    outgoing = pl.pallas_call(
        pack_kernel,
        out_shape=shape(DEVICES * CHUNK, CELLS),
        in_specs=[raw] * 4,
        out_specs=vmem(),
        scratch_shapes=[
            pltpu.VMEM((BANDS * PROBES, CELLS), jnp.float32),
            pltpu.VMEM((BANDS * PROBES, CELLS), jnp.float32),
            pltpu.VMEM((STRAINS, ROWS, CELLS // ROWS), jnp.float32),
            pltpu.VMEM((BANDS, CELLS), jnp.float32),
            pltpu.SemaphoreType.DMA((4,)),
        ],
        compiler_params=params(8),
        name="pack",
    )(
        far(probes.reshape(BANDS * PROBES, CELLS)),
        far(test_block.reshape(BANDS * PROBES, CELLS)),
        far(jnp.transpose(strain_elastic[0], (1, 0, 2))),
        far(band_edge.reshape(BANDS, CELLS)),
    )
    mine = exchange(outgoing, CHUNK)
    other = lax.ppermute(mine, "cuts", [(i, i ^ 1) for i in range(cut_count)])
    scale = (cut_count * BANDS * ROWS * CELLS) ** (-0.5)
    cosines, wave, spread, turns = constants()
    wide = SLICES * BANDS

    def prepare(*refs):
        prepare_kernel(cosines, *refs)

    prepared = pl.pallas_call(
        prepare,
        out_shape=(
            shape(ROWS, STRAINS * SLICES, PTS * CELLS),
            shape(ROWS, SLICES, PTS * CELLS),
            shape(ROWS * PTS * SLICES, CELLS),
            shape(SLICES, PLANE),
            shape(ROWS, SLICES, CELLS),
            jax.ShapeDtypeStruct((PLANE, PLANE), jnp.bfloat16),
            jax.ShapeDtypeStruct(turns.shape, turns.dtype),
        ),
        in_specs=[raw] * 6 + [vmem()] * 2,
        out_specs=(vmem(),) * 7,
        scratch_shapes=[
            pltpu.SMEM(slice_hop.shape, jnp.float32),
            pltpu.SMEM(cross_hop.shape, jnp.float32),
            pltpu.SMEM(deform.shape, jnp.float32),
            pltpu.SMEM(strain_ids.shape, jnp.int32),
            pltpu.VMEM(spread.shape, jnp.float32),
            pltpu.SemaphoreType.DMA((6,)),
            pltpu.VMEM((3 * wide, PLANE), jnp.bfloat16),
            pltpu.VMEM((TERMS * SLICES, PASSES * wide), jnp.bfloat16),
            pltpu.VMEM((ROWS, wide, CELLS), jnp.float32),
            pltpu.VMEM((PASSES * wide, PTS * CELLS), jnp.bfloat16),
            pltpu.VMEM((wide, CELLS), jnp.float32),
            pltpu.VMEM((wide, CELLS), jnp.float32),
            pltpu.VMEM((ROWS, 2 * SLICES, PTS * CELLS), jnp.float32),
            pltpu.VMEM((BANDS, CELLS), jnp.float32),
            pltpu.VMEM((ROWS * PTS * SLICES, CELLS), jnp.bfloat16),
        ],
        compiler_params=params(20),
        name="prepare",
    )(
        *map(far, (slice_hop, cross_hop, deform, strain_ids, spread, turns)), mine, wave
    )

    def main(*refs):
        main_kernel(scale, *refs)

    blocks = pl.pallas_call(
        main,
        out_shape=shape(DEVICES * BACK, CELLS),
        in_specs=[vmem()] * 9,
        out_specs=vmem(),
        scratch_shapes=[
            pltpu.VMEM((STRAINS * SLICES, PLANE), jnp.bfloat16),
            pltpu.VMEM((STRAINS * SLICES, PLANE), jnp.bfloat16),
            pltpu.VMEM((STRAINS * SLICES, PLANE), jnp.float32),
            pltpu.VMEM((3 * SLICES, NMOM * PLANE), jnp.bfloat16),
            pltpu.VMEM((SLICES, NMOM * PLANE), jnp.float32),
            pltpu.VMEM((NMOM * ROWS, SLICES, CELLS), jnp.float32),
        ],
        compiler_params=params(20),
        name="solve",
    )(mine, other, *prepared)
    fields, projected = pl.pallas_call(
        gather_kernel,
        out_shape=(shape(2, 2, BANDS * PROBES, CELLS), shape(NMOM, 2, PROBES, PROBES)),
        in_specs=[vmem()],
        out_specs=(vmem(), vmem()),
        compiler_params=params(8),
        name="gather",
    )(exchange(blocks, BACK))
    return fields.reshape(2, 2, 1, BANDS, PROBES, 1, CELLS), projected


def solution(mesh):
    placed = (
        P("cuts", None, None, "tile", None),
        P("cuts", None, None, "tile", None),
        P(None, "tile", None),
        P(),
        P(),
        P(),
        P("cuts", "tile", None, None),
        P(),
    )
    return jax.shard_map(
        on_device,
        mesh=mesh,
        in_specs=placed,
        out_specs=(P(None, None, "cuts", None, None, "tile", None), P()),
        check_vma=False,
    )
```
